32 devices in a mesh: row: 4 (over z), col: 8 (over y, x, core).
Axes of the slice: x: 2, y: 2, z: 4, core: 2. Of those that a mesh axis runs over, the one named last changes fastest.
Arguments:
- splat_params: float32 [10, 2097152], P(None, ('row', 'col')), as said below
- list_owner: int32 [128, 1024, 1], P(('row', 'col')), may hold values from 0 to 31; in each aligned block of 4096 rows (0 to 4095, 4096 to 8191, ..., all dimensions but the last counted through in order) at most 256 rows name the same one
- list_slot: int32 [128, 1024], P(('row', 'col')), may hold values from 0 to 65535
- list_length: int32 [128], P(('row', 'col')), may hold values from 512 to 1024, as said below
- target: float32 [4, 128, 256], P(None, ('row', 'col')), may hold values from 0 to 1
Outputs:
- rendered: float32 [4, 128, 256], P(None, ('row', 'col'))
- splat_grads: float32 [10, 2097152], P(None, ('row', 'col'))
The draws below stay inside these ranges and needn't reach their ends.
Inputs may be any that keep to these rules, and one draw needn't show every extreme that they name: `list_owner`: within the entries of one device's tiles (aligned blocks of 4096 entries), no owner is named more than 256 times, a bound that some block reaches. `list_length`: some tile has exactly 1024 live entries; every tile has at least 512. `splat_params`: conic entries satisfy a > 0, c > 0 and b * b < a * c; opacity lies in (0, 0.02]; colours and depth lie in [0, 1].
All inputs are finite; a program needn't handle non-finite values.
Results may differ from the reference program's by a relative error of at most 0.0003.
Values sent between devices are 32-bit elements; how exact they have to be, the bound alone decides.
A program may use at most 128 MiB of HBM per device.

```python
import math
import jax
import jax.numpy as jnp
import numpy as np
from jax import lax

SIDE = 16
PIX = 256
K = 1024
TILE_DEV = 4
G_DEV = 65536
TILES = 128
GROUP_TILES = 32
SPLATS = 2097152
CAP = 256
DEVICES = 32


def log_uniform(key, shape, low, high):
    return jnp.exp(jax.random.uniform(key, shape, jnp.float32, jnp.log(low), jnp.log(high)))


def draw_splat_params(key, part):
    keys = jax.random.split(key, 8)
    shape = (SPLATS,)
    mean_x = jax.random.uniform(keys[0], shape, jnp.float32, -2.0, 18.0)
    mean_y = jax.random.uniform(keys[1], shape, jnp.float32, -2.0, 18.0)
    conic_a = log_uniform(keys[2], shape, 0.05, 0.5)
    conic_c = log_uniform(keys[3], shape, 0.05, 0.5)
    conic_b = jax.random.uniform(keys[4], shape, jnp.float32, -0.6, 0.6) * jnp.sqrt(conic_a * conic_c)
    opacity = log_uniform(keys[5], shape, 0.002, 0.02)
    colours = jax.random.uniform(keys[6], (3, SPLATS), jnp.float32)
    depth = log_uniform(keys[7], shape, 0.05, 1.0)
    geometry = jnp.stack([mean_x, mean_y, conic_a, conic_b, conic_c, opacity])
    return jnp.concatenate([geometry, colours, depth[None, :]], axis=0)


def draw_list_length(key, part):
    tile_index = jnp.arange(TILES, dtype=jnp.int32)
    groups = TILES // GROUP_TILES
    group = tile_index // GROUP_TILES
    heavy = jax.random.randint(jax.random.fold_in(key, 11), (), 0, groups)
    is_heavy = group == heavy
    longest = jnp.where(is_heavy, K, 3 * K // 4).astype(jnp.int32)
    shortest = jnp.where(is_heavy, 7 * K // 8, K // 2).astype(jnp.int32)
    lengths = jax.random.randint(jax.random.fold_in(key, 12), (TILES,), shortest, longest + 1)
    return jnp.where(tile_index == heavy * GROUP_TILES, K, lengths).astype(jnp.int32)


def place_ends(array, rng, least, high):
    dims = array.shape
    spot = [jax.random.randint(jax.random.fold_in(rng, axis), (), 0, dims[axis]) for axis in range(len(dims))]
    array = array.at[tuple(spot)].set(least)
    longest = dims.index(max(dims))
    spot[longest] = (spot[longest] + 1) % dims[longest]
    return array.at[tuple(spot)].set(high)


def block_scale(own_key, dims, cuts, low, top_value):
    factor_of = 1.0
    for axis_at, blocks in cuts:
        draws = jax.random.uniform(jax.random.fold_in(jax.random.fold_in(own_key, 6), axis_at), (blocks,), jnp.float32, low / len(cuts), top_value / len(cuts))
        factor_of = factor_of * jnp.repeat(jnp.exp(draws), dims[axis_at] // blocks).reshape((-1,) + (1,) * (len(dims) - 1 - axis_at))
    return factor_of


def shared_out(rng, own, number, rows, count, top, most, lean):
    order = jax.random.permutation(rng, count)
    crowded, common = shares(count, rows * top, most, lean, True), shares(count, rows * top, most, lean, False)
    places = jnp.arange(count)

    def named(sizes, turn):
        used = int((sizes > 0).sum())
        fixed = max(1, used // 4)
        moved = fixed + (places - fixed + turn * (used - fixed)) % max(1, count - fixed)
        return jnp.zeros((count,), jnp.int32).at[order[jnp.where(places < fixed, places, moved)]].set(jnp.asarray(sizes, jnp.int32))

    sizes = jnp.where(number % 4 == 0, named(crowded, number // 4), named(common, number - number // 4 - 1))
    mixed = jax.random.permutation(jax.random.fold_in(own, 3), count)
    source_of, receiver = mixed[0:count // 2 * 2:2], mixed[1:count // 2 * 2:2]
    slack = jnp.minimum(sizes[source_of] - 1, most - sizes[receiver]) // 2
    slack = jnp.where((source_of == order[0]) | (receiver == order[0]) | (sizes[receiver] == 0), 0, jnp.maximum(slack, 0))
    moved = jax.random.randint(jax.random.fold_in(own, 4), (count // 2,), 0, 1 << 20) % (slack + 1)
    sizes = sizes.at[source_of].add(-moved).at[receiver].add(moved)
    labels = jnp.searchsorted(jnp.cumsum(sizes), jnp.arange(rows * top), side="right").astype(jnp.int32)
    table = labels.reshape(top, rows).T
    table = table[jax.random.permutation(jax.random.fold_in(own, 1), rows)]
    turn = jax.random.randint(jax.random.fold_in(own, 2), (rows, 1), 0, top)
    return jnp.take_along_axis(table, (jnp.arange(top)[None, :] + turn) % top, axis=1)


def shares(amount, total, most, skew, full):
    loads = [(1 << 20) // math.isqrt(standing ** skew) + 1 for standing in range(1, amount + 1)]
    largest = most if full else min(most, max(-(-total // amount), total * loads[0] // sum(loads)))
    least = 1 if total - largest >= amount - 1 else 0
    counts, rest = [largest] + [least] * (amount - 1), total - largest - least * (amount - 1)
    while rest > 0:
        free = [i for i in range(1, amount) if counts[i] < largest] or [i for i in range(1, amount) if counts[i] < most]
        whole, left = sum([loads[i] for i in free]), rest
        for i in free:
            extra = min(most - counts[i], max(1, left * loads[i] // whole), rest)
            counts[i] = counts[i] + extra
            rest = rest - extra
    return np.array(counts)


def setup_inputs(seed: int = 0) -> dict:
    seeds = jax.random.split(jax.random.key(seed), 6)
    splat_params = draw_splat_params(jax.random.fold_in(seeds[5], 71), 0)
    list_owner_keys = jax.random.split(jax.random.fold_in(seeds[1], 1), TILES * K // (TILE_DEV * K))
    list_owner_turns = jax.random.permutation(jax.random.fold_in(seeds[1], 3), TILES * K // (TILE_DEV * K))
    list_owner = jax.vmap(lambda own, number: shared_out(jax.random.fold_in(seeds[1], 2), own, number, TILE_DEV * K, DEVICES, 1, CAP, 2))(list_owner_keys, list_owner_turns).reshape((TILES, K, 1))
    list_slot = place_ends(jax.random.randint(seeds[2], (TILES, K), 0, G_DEV), jax.random.fold_in(seeds[2], 1), 0, G_DEV - 1).astype(jnp.int32)
    list_length = draw_list_length(jax.random.fold_in(seeds[5], 71), 0)
    target = jnp.clip(1.0 * jax.random.uniform(seeds[4], (4, TILES, PIX), jnp.float32) ** block_scale(seeds[4], (4, TILES, PIX), ((1, 32),), -0.2, 0.2), 0.0, 1.0)
    return dict(splat_params=splat_params, list_owner=list_owner, list_slot=list_slot, list_length=list_length, target=target)


precise = lax.Precision.HIGHEST


def render_tile(values, length, tile_target):
    pixel_index = jnp.arange(PIX)
    pixel_x = (pixel_index % SIDE).astype(jnp.float32) + 0.5
    pixel_y = (pixel_index // SIDE).astype(jnp.float32) + 0.5
    live_mask = (jnp.arange(K) < length).astype(jnp.float32)
    mean_x = values[0]
    mean_y = values[1]
    conic_a = values[2]
    conic_b = values[3]
    conic_c = values[4]
    opacity = values[5] * live_mask
    colours = values[6:10]
    offset_x = pixel_x[:, None] - mean_x[None, :]
    offset_y = pixel_y[:, None] - mean_y[None, :]
    exponent = 0.5 * (conic_a * offset_x * offset_x + conic_c * offset_y * offset_y) + conic_b * offset_x * offset_y
    falloff = jnp.exp(-exponent)
    alphas = opacity[None, :] * falloff
    log_keep = jnp.log1p(-alphas)
    log_trans = jnp.cumsum(log_keep, axis=1) - log_keep
    transmit = jnp.exp(log_trans)
    weight = alphas * transmit
    rendered = jnp.dot(colours, weight.T, precision=precise)
    grad_image = 2.0 * (rendered - tile_target)
    grad_colours = jnp.dot(grad_image, weight, precision=precise)
    shading = jnp.dot(grad_image.T, colours, precision=precise)
    spent_sum = weight * shading
    before = jnp.cumsum(spent_sum, axis=1)
    grand_total = jnp.sum(grad_image * rendered, axis=0)
    grad_alpha = transmit * shading - (grand_total[:, None] - before) / (1.0 - alphas)
    grad_power = -grad_alpha * alphas
    grad_mean_x = jnp.sum(-grad_power * (conic_a * offset_x + conic_b * offset_y), axis=0)
    grad_mean_y = jnp.sum(-grad_power * (conic_c * offset_y + conic_b * offset_x), axis=0)
    grad_a = jnp.sum(grad_power * 0.5 * offset_x * offset_x, axis=0)
    grad_b = jnp.sum(grad_power * offset_x * offset_y, axis=0)
    grad_c = jnp.sum(grad_power * 0.5 * offset_y * offset_y, axis=0)
    grad_opacity = jnp.sum(grad_alpha * falloff, axis=0) * live_mask
    geometry_grads = jnp.stack([grad_mean_x, grad_mean_y, grad_a, grad_b, grad_c, grad_opacity])
    return rendered, jnp.concatenate([geometry_grads, grad_colours], axis=0)


def reference(splat_params, list_owner, list_slot, list_length, target):
    splat_ids = (list_owner[:, :, 0] * G_DEV + list_slot).astype(jnp.int32)

    def render_one(tile_step):
        values = jnp.take(splat_params, splat_ids[tile_step], axis=1)
        return render_tile(values, list_length[tile_step], target[:, tile_step, :])

    images, entry_grads = lax.map(render_one, jnp.arange(TILES, dtype=jnp.int32))
    rendered = jnp.transpose(images, (1, 0, 2))
    flat_grads = jnp.transpose(entry_grads, (1, 0, 2)).reshape(10, TILES * K)
    splat_grads = jnp.zeros((10, SPLATS), jnp.float32).at[:, splat_ids.reshape(-1)].add(flat_grads)
    return rendered, splat_grads
```

```python
import functools

import jax
import jax.numpy as jnp
from jax import lax
from jax.experimental import pallas as pl
from jax.experimental.pallas import tpu as pltpu
from jax.sharding import PartitionSpec as P

SIDE = 16
SB = 256
LANES = 256
CH = 10
F32 = jnp.float32
BF16 = jnp.bfloat16
NT = (((1,), (1,)), ((), ()))


def iota(shape, dim):
    return lax.broadcasted_iota(jnp.int32, shape, dim)


def split(x):
    high = x.astype(BF16)
    return high, (x - high.astype(F32)).astype(BF16)


def mm(a, b):
    return jnp.dot(a, b, preferred_element_type=F32)


def mm_nt(a, b):
    return lax.dot_general(a, b, NT, preferred_element_type=F32)


def one_hot(index, size):
    return jnp.where(iota((size, index.shape[1]), 0) == index, 1.0, 0.0).astype(BF16)


def plan_kernel(length_ref, own_ref, slot_ref, req_ref, rank_ref, live_ref):
    devices, cap = req_ref.shape
    entries = own_ref.shape[1]
    slots = entries // length_ref.shape[0]
    strict = jnp.where(iota((SB, SB), 0) < iota((SB, SB), 1), 1.0, 0.0).astype(BF16)
    carry = jnp.zeros((devices, 1), F32)
    high = jnp.zeros((devices, cap), F32)
    low = jnp.zeros((devices, cap), F32)
    for j in range(entries // SB):
        part = slice(j * SB, (j + 1) * SB)
        place = iota((1, SB), 1) + (j * SB) % slots
        owner = jnp.where(place < length_ref[j * SB // slots], own_ref[:, part], -1)
        live_ref[:, part] = owner
        mine = iota((devices, SB), 0) == owner
        ones = jnp.where(mine, 1.0, 0.0)
        count = mm(ones.astype(BF16), strict) + carry
        rank = jnp.sum(ones * count, axis=0, keepdims=True).astype(jnp.int32)
        carry = carry + jnp.sum(ones, axis=1, keepdims=True)
        rank_ref[:, part] = rank
        named = slot_ref[:, part]
        places = one_hot(rank, cap)
        slot_high = (named >> 8).astype(F32)
        slot_low = ((named & 255) + 1).astype(F32)
        high = high + mm_nt(jnp.where(mine, slot_high, 0.0).astype(BF16), places)
        low = low + mm_nt(jnp.where(mine, slot_low, 0.0).astype(BF16), places)
    req_ref[...] = (high * 256.0 + low).astype(jnp.int32) - 1


def prepare_kernel(params_ref, table_ref, wide_ref):
    rows = table_ref.shape[0]
    block = wide_ref.shape[1]
    wide_ref[...] = jnp.zeros_like(wide_ref)

    def step(j, _):
        for k in range(8):
            at = pl.ds(pl.multiple_of(k * rows + j * block, block), block)
            wide_ref[k * 16 : k * 16 + CH, :] = params_ref[:, at]
        table_ref[pl.ds(pl.multiple_of(j * block, block), block), :] = jnp.transpose(wide_ref[...])
        return 0

    lax.fori_loop(0, rows // block, step, 0)


def lookup_kernel(row_ref, ask_ref, table_ref, out_ref, even_ref, odd_ref):
    rows = table_ref.shape[0]
    width = ask_ref.shape[1]
    steps = ask_ref.shape[0]
    cap = out_ref.shape[2]
    shift = rows.bit_length() - 1
    eye = jnp.where(iota((128, 128), 0) == iota((128, 128), 1), 1.0, 0.0).astype(BF16)

    def fetch(step, held):
        for j in range(width):
            held[j : j + 1, :] = table_ref[pl.ds(row_ref[step * width + j], 1), :]

    def pick(step, held):
        high, low = split(held[...])
        turned = mm_nt(eye, high) + mm_nt(eye, low)
        group = ask_ref[pl.ds(step, 1), :] >> shift
        found = jnp.zeros((16, width), F32)
        for k in range(8):
            found = found + jnp.where(group == k, turned[k * 16 : k * 16 + 16], 0.0)
        for k in range(width // cap):
            out_ref[step * (width // cap) + k] = found[:CH, k * cap : (k + 1) * cap]

    fetch(0, even_ref)

    def pair(p, _):
        step = 2 * p
        fetch(step + 1, odd_ref)
        pick(step, even_ref)
        fetch(lax.rem(step + 2, steps), even_ref)
        pick(step + 1, odd_ref)
        return 0

    lax.fori_loop(0, steps // 2, pair, 0)


def render_kernel(
    length_ref, own_ref, rank_ref, reply_ref, target_ref, image_ref, out_ref,
    vals, grads, falloff_ref, trans_ref, high_ref, low_ref, shade_ref, before_ref, pack_ref,
):
    tile = pl.program_id(0)
    devices = reply_ref.shape[0] // CH
    cap = reply_ref.shape[1]
    slots = own_ref.shape[2]
    pixels = target_ref.shape[2]
    blocks = slots // SB
    length = length_ref[tile]
    mine = iota((devices, slots), 0) == own_ref[0]
    places = one_hot(rank_ref[0], cap)
    reply_high, reply_low = split(reply_ref[...])
    fetched = mm(reply_high, places) + mm(reply_low, places)
    vals[...] = jnp.zeros_like(vals)
    live = jnp.where(iota((1, slots), 1) < length, 1.0, 0.0)
    for ch in range(CH):
        part = slice(ch * devices, (ch + 1) * devices)
        value = jnp.sum(jnp.where(mine, fetched[part], 0.0), axis=0, keepdims=True)
        if ch == 5:
            value = value * live
        row = ch if ch < 6 else ch + 2
        vals[row : row + 1, :] = value

    strict = jnp.where(iota((SB, SB), 0) < iota((SB, SB), 1), 1.0, 0.0).astype(BF16)
    inclusive = jnp.where(iota((SB, SB), 0) <= iota((SB, SB), 1), 1.0, 0.0).astype(BF16)
    centres = iota((SIDE, SB), 0).astype(F32) + 0.5
    side_rows = pixels // SIDE

    carry = jnp.zeros((pixels, 1), F32)
    image = jnp.zeros((pixels, 8), F32)
    for blk in range(blocks):
        at = slice(blk * SB, (blk + 1) * SB)
        dx = centres - vals[0:1, at]
        dy = centres - vals[1:2, at]
        ex = 0.5 * vals[2:3, at] * dx * dx
        ey = 0.5 * vals[4:5, at] * dy * dy
        bdy = vals[3:4, at] * dy
        opacity = vals[5:6, at]
        for y in range(side_rows):
            rows = slice(y * SIDE, (y + 1) * SIDE)
            exponent = ex + ey[y : y + 1] + dx * bdy[y : y + 1]
            falloff = jnp.exp(-exponent)
            falloff_ref[rows, at] = falloff
            keep = jnp.log(1.0 - opacity * falloff)
            high, low = split(keep)
            high_ref[rows, :] = high
            low_ref[rows, :] = low
        total = mm(high_ref[...], strict) + mm(low_ref[...], strict) + carry
        last = high_ref[:, SB - 128 :].astype(F32) + low_ref[:, SB - 128 :].astype(F32)
        carry = total[:, SB - 1 : SB] + last[:, 127:128]
        trans = jnp.exp(total)
        trans_ref[:, at] = trans
        weight_high, weight_low = split(trans * (opacity * falloff_ref[:, at]))
        colour_high, colour_low = split(vals[8:16, at])
        image = image + (
            mm_nt(weight_high, colour_high)
            + mm_nt(weight_high, colour_low)
            + mm_nt(weight_low, colour_high)
        )
    rendered = jnp.transpose(image)
    image_ref[0] = rendered
    grad_image = 2.0 * (rendered - target_ref[0])
    grad_high, grad_low = split(grad_image)
    grad_wide = grad_high.astype(F32)
    grad_rest = grad_image - grad_wide
    turned = jnp.transpose(jnp.concatenate([grad_wide, grad_wide, grad_rest, grad_image], axis=0))
    turned_parts = turned.astype(BF16)
    grand_total = jnp.sum(jnp.transpose(grad_image) * image, axis=1, keepdims=True)

    spent = jnp.zeros((pixels, 1), F32)
    for blk in range(blocks):
        at = slice(blk * SB, (blk + 1) * SB)
        mean_x, mean_y = vals[0:1, at], vals[1:2, at]
        conic_a, conic_b, conic_c = vals[2:3, at], vals[3:4, at], vals[4:5, at]
        opacity = vals[5:6, at]
        dx = centres - mean_x
        dy = centres - mean_y
        colours = vals[8:16, at]
        colour_wide = colours.astype(BF16).astype(F32)
        colour_parts = jnp.concatenate(
            [colour_wide, colours - colour_wide, colour_wide, jnp.zeros_like(colours)], axis=0
        ).astype(BF16)
        shading = mm(turned_parts, colour_parts)
        shade_ref[...] = shading
        weight = trans_ref[:, at] * (opacity * falloff_ref[:, at])
        weight_high, weight_low = split(weight)
        grads[8:16, at] = (
            mm(grad_high, weight_high) + mm(grad_low, weight_high) + mm(grad_high, weight_low)
        )
        high, low = split(weight * shading)
        before = mm(high, inclusive) + mm(low, inclusive) + spent
        spent = before[:, SB - 1 : SB]
        before_ref[...] = grand_total - before
        power0 = jnp.zeros((SIDE, SB), F32)
        power1 = power0
        power2 = power0
        opaque = power0
        for y in range(side_rows):
            rows = slice(y * SIDE, (y + 1) * SIDE)
            falloff = falloff_ref[rows, at]
            alpha = opacity * falloff
            grad_alpha = trans_ref[rows, at] * shade_ref[rows, :] - before_ref[rows, :] / (
                1.0 - alpha
            )
            opaque = opaque + grad_alpha * falloff
            power = grad_alpha * alpha
            power0 = power0 - power
            moment = power * dy[y : y + 1]
            power1 = power1 - moment
            power2 = power2 - moment * dy[y : y + 1]
        across = power0 * dx
        sum_x = jnp.sum(across, axis=0, keepdims=True)
        sum_y = jnp.sum(power1, axis=0, keepdims=True)
        grads[0:1, at] = -(conic_a * sum_x + conic_b * sum_y)
        grads[1:2, at] = -(conic_c * sum_y + conic_b * sum_x)
        grads[2:3, at] = 0.5 * jnp.sum(across * dx, axis=0, keepdims=True)
        grads[3:4, at] = jnp.sum(power1 * dx, axis=0, keepdims=True)
        grads[4:5, at] = 0.5 * jnp.sum(power2, axis=0, keepdims=True)
        grads[5:6, at] = jnp.sum(opaque, axis=0, keepdims=True) * live[:, at]

    for ch in range(CH):
        part = slice(ch * devices, (ch + 1) * devices)
        row = ch if ch < 6 else ch + 2
        high, low = split(jnp.where(mine, grads[row : row + 1, :], 0.0))
        pack_ref[0, part, :] = high
        pack_ref[1, part, :] = low
    sent = mm_nt(pack_ref[0], places) + mm_nt(pack_ref[1], places)

    @pl.when(tile == 0)
    def _():
        out_ref[...] = sent

    @pl.when(tile > 0)
    def _():
        out_ref[...] += sent


def scatter_kernel(row_ref, count_ref, ask_ref, grad_ref, out_ref, wide_ref, *banks):
    rows = banks[0].shape[0]
    devices, _, cap = grad_ref.shape
    width = ask_ref.shape[1]
    steps = ask_ref.shape[0]
    shift = rows.bit_length() - 1
    unit = 256

    def clear(j, _):
        at = pl.ds(pl.multiple_of(j * unit, unit), unit)
        for bank in banks:
            bank[at, :] = jnp.zeros((unit, 128), F32)
        return 0

    lax.fori_loop(0, rows // unit, clear, 0)

    def widen(step, _):
        group = ask_ref[pl.ds(step, 1), :] >> shift
        parts = [grad_ref[step * (width // cap) + k] for k in range(width // cap)]
        grad = jnp.concatenate(parts, axis=1) if len(parts) > 1 else parts[0]
        grad = jnp.concatenate([grad, jnp.zeros((16 - CH, width), F32)], axis=0)
        wide = jnp.concatenate([jnp.where(group == k, grad, 0.0) for k in range(8)], axis=0)
        wide_ref[pl.ds(pl.multiple_of(step * width, width), width), :] = jnp.transpose(wide)
        return 0

    lax.fori_loop(0, steps, widen, 0)
    burst = 16

    def source(s, _):
        def add(j, _):
            base = s * cap + j * burst
            lines = wide_ref[pl.ds(pl.multiple_of(base, burst), burst), :]
            for u in range(burst):
                bank = banks[u % len(banks)]
                at = pl.ds(row_ref[base + u], 1)
                bank[at, :] = bank[at, :] + lines[u : u + 1]
            return 0

        return lax.fori_loop(0, (count_ref[s] + burst - 1) // burst, add, 0)

    lax.fori_loop(0, devices, source, 0)
    block = 512

    def finish(j, _):
        at = pl.ds(pl.multiple_of(j * block, block), block)
        total = banks[0][at, :]
        for bank in banks[1:]:
            total = total + bank[at, :]
        turned = jnp.transpose(total)
        for k in range(8):
            to = pl.ds(pl.multiple_of(k * rows + j * block, block), block)
            out_ref[:, to] = turned[k * 16 : k * 16 + CH]
        return 0

    lax.fori_loop(0, rows // block, finish, 0)


def body(splat_params, list_owner, list_slot, list_length, target):
    devices = lax.axis_size(("row", "col"))
    tiles, slots = list_slot.shape
    entries = tiles * slots
    splats = splat_params.shape[1]
    pixels = target.shape[2]
    cap = 2 * entries // devices
    total = devices * cap
    rows = splats // 8
    smem = pl.BlockSpec(memory_space=pltpu.SMEM)
    vmem = pl.BlockSpec(memory_space=pltpu.VMEM)
    owners = list_owner.reshape(1, entries)
    requests, ranks, living = pl.pallas_call(
        plan_kernel,
        in_specs=[smem, vmem, vmem],
        out_shape=(
            jax.ShapeDtypeStruct((devices, cap), jnp.int32),
            jax.ShapeDtypeStruct((1, entries), jnp.int32),
            jax.ShapeDtypeStruct((1, entries), jnp.int32),
        ),
        name="plan",
    )(list_length, owners, list_slot.reshape(1, entries))
    asked = lax.all_to_all(requests, ("row", "col"), split_axis=0, concat_axis=0, tiled=True)
    table = pl.pallas_call(
        prepare_kernel,
        out_shape=jax.ShapeDtypeStruct((rows, 128), F32),
        scratch_shapes=[pltpu.VMEM((128, 512), F32)],
        cost_estimate=pl.CostEstimate(flops=0, bytes_accessed=8 * CH * splats, transcendentals=0),
        name="prepare",
    )(splat_params)
    steps = total // LANES
    lines = (asked & (rows - 1)).reshape(total)
    counts = jnp.sum((asked >= 0).astype(jnp.int32), axis=1)
    groups = asked.reshape(steps, LANES)
    looked = pl.pallas_call(
        lookup_kernel,
        in_specs=[smem, vmem, vmem],
        out_shape=jax.ShapeDtypeStruct((devices, CH, cap), F32),
        scratch_shapes=[pltpu.VMEM((LANES, 128), F32)] * 2,
        name="lookup",
    )(lines, groups, table)
    answer = lax.all_to_all(looked, ("row", "col"), split_axis=0, concat_axis=0, tiled=True)
    replies = answer.transpose(1, 0, 2).reshape(CH * devices, cap)
    targets = jnp.pad(target.transpose(1, 0, 2), ((0, 0), (0, 4), (0, 0)))
    images, outgoing = pl.pallas_call(
        render_kernel,
        grid=(tiles,),
        in_specs=[
            pl.BlockSpec(memory_space=pltpu.SMEM),
            pl.BlockSpec((1, 1, slots), lambda i: (i, 0, 0)),
            pl.BlockSpec((1, 1, slots), lambda i: (i, 0, 0)),
            pl.BlockSpec((CH * devices, cap), lambda i: (0, 0)),
            pl.BlockSpec((1, 8, pixels), lambda i: (i, 0, 0)),
        ],
        out_specs=(
            pl.BlockSpec((1, 8, pixels), lambda i: (i, 0, 0)),
            pl.BlockSpec((CH * devices, cap), lambda i: (0, 0)),
        ),
        out_shape=(
            jax.ShapeDtypeStruct((tiles, 8, pixels), F32),
            jax.ShapeDtypeStruct((CH * devices, cap), F32),
        ),
        scratch_shapes=[
            pltpu.VMEM((16, slots), F32),
            pltpu.VMEM((16, slots), F32),
            pltpu.VMEM((pixels, slots), F32),
            pltpu.VMEM((pixels, slots), F32),
            pltpu.VMEM((pixels, SB), BF16),
            pltpu.VMEM((pixels, SB), BF16),
            pltpu.VMEM((pixels, SB), F32),
            pltpu.VMEM((pixels, SB), F32),
            pltpu.VMEM((2, CH * devices, slots), BF16),
        ],
        name="render",
    )(
        list_length,
        living.reshape(tiles, 1, slots),
        ranks.reshape(tiles, 1, slots),
        replies,
        targets,
    )
    rendered = images[:, :4].transpose(1, 0, 2)
    sending = outgoing.reshape(CH, devices, cap).transpose(1, 0, 2)
    incoming = lax.all_to_all(sending, ("row", "col"), split_axis=0, concat_axis=0, tiled=True)
    splat_grads = pl.pallas_call(
        scatter_kernel,
        in_specs=[smem, smem, vmem, vmem],
        out_shape=jax.ShapeDtypeStruct((CH, splats), F32),
        scratch_shapes=[pltpu.VMEM((total, 128), F32)] + [pltpu.VMEM((rows, 128), F32)] * 4,
        name="accumulate",
    )(lines, counts, groups, incoming)
    return (rendered, splat_grads)


def solution(mesh):
    in_specs = (
        P(None, ("row", "col")),
        P(("row", "col"), None, None),
        P(("row", "col"), None),
        P(("row", "col")),
        P(None, ("row", "col"), None),
    )
    out_specs = (P(None, ("row", "col"), None), P(None, ("row", "col")))
    return jax.shard_map(body, mesh=mesh, in_specs=in_specs, out_specs=out_specs, check_vma=False)
```

```python
import functools

import jax
import jax.numpy as jnp
from jax import lax
from jax.experimental import pallas as pl
from jax.experimental.pallas import tpu as pltpu
from jax.sharding import PartitionSpec as P

SIDE = 16
SB = 256
LANES = 256
CH = 10
F32 = jnp.float32
BF16 = jnp.bfloat16
NT = (((1,), (1,)), ((), ()))


def iota(shape, dim):
    return lax.broadcasted_iota(jnp.int32, shape, dim)


def split(x):
    high = x.astype(BF16)
    return high, (x - high.astype(F32)).astype(BF16)


def mm(a, b):
    return jnp.dot(a, b, preferred_element_type=F32)


def mm_nt(a, b):
    return lax.dot_general(a, b, NT, preferred_element_type=F32)


def one_hot(index, size):
    return jnp.where(iota((size, index.shape[1]), 0) == index, 1.0, 0.0).astype(BF16)


def step_kernel(
    length_ref, own_ref, slot_ref, target_ref, params_hbm, image_ref, asked_ref, incoming_ref,
    params_ref, table_ref, wide_ref, even_ref, odd_ref, lines_ref, live_ref, rank_ref, req_ref,
    found_ref, replies_ref, outgoing_ref, reply_high, reply_low, sent_ref,
    vals, grads, falloff_ref, trans_ref, high_ref, low_ref, shade_ref, before_ref, pack_ref,
    local_sem, send_sem, recv_sem,
):
    rows_on = lax.axis_size("row")
    cols_on = lax.axis_size("col")
    devices = rows_on * cols_on
    me = lax.axis_index("row") * cols_on + lax.axis_index("col")
    tiles, slots = slot_ref.shape
    cap = found_ref.shape[2]
    pixels = target_ref.shape[2]
    rows = table_ref.shape[0]
    shift = rows.bit_length() - 1
    others = pl.ds(0, devices - 1)

    def peer(k):
        return lax.rem(me + k, devices)

    def place_of(device):
        return (device // cols_on, lax.rem(device, cols_on))

    def push(device, source, target, phase):
        return pltpu.make_async_remote_copy(
            src_ref=source.at[device],
            dst_ref=target.at[me],
            send_sem=send_sem.at[phase],
            recv_sem=recv_sem.at[phase],
            device_id=place_of(device),
            device_id_type=pl.DeviceIdType.MESH,
        )

    def drain(source, target, phase):
        pltpu.make_async_copy(target.at[others], target.at[others], recv_sem.at[phase]).wait()
        pltpu.make_async_copy(source.at[others], source.at[others], send_sem.at[phase]).wait()

    barrier = pltpu.get_barrier_semaphore()

    @pl.loop(1, devices)
    def _(k):
        pl.semaphore_signal(
            barrier, inc=1, device_id=place_of(peer(k)), device_id_type=pl.DeviceIdType.MESH
        )

    load = pltpu.make_async_copy(params_hbm, params_ref, local_sem.at[0])
    load.start()

    strict = jnp.where(iota((SB, SB), 0) < iota((SB, SB), 1), 1.0, 0.0).astype(BF16)
    inclusive = jnp.where(iota((SB, SB), 0) <= iota((SB, SB), 1), 1.0, 0.0).astype(BF16)
    count = jnp.zeros((devices, 1), F32)
    high = jnp.zeros((devices, cap), F32)
    low = jnp.zeros((devices, cap), F32)
    for tile in range(tiles):
        for j in range(slots // SB):
            part = slice(j * SB, (j + 1) * SB)
            owner = jnp.where(iota((1, SB), 1) + j * SB < length_ref[tile], own_ref[tile, :, part], -1)
            live_ref[tile, :, part] = owner
            mine = iota((devices, SB), 0) == owner
            ones = jnp.where(mine, 1.0, 0.0)
            ahead = mm(ones.astype(BF16), strict) + count
            rank = jnp.sum(ones * ahead, axis=0, keepdims=True).astype(jnp.int32)
            count = count + jnp.sum(ones, axis=1, keepdims=True)
            rank_ref[tile, :, part] = rank
            named = slot_ref[tile : tile + 1, part]
            places = one_hot(rank, cap)
            slot_high = (named >> 8).astype(F32)
            slot_low = ((named & 255) + 1).astype(F32)
            high = high + mm_nt(jnp.where(mine, slot_high, 0.0).astype(BF16), places)
            low = low + mm_nt(jnp.where(mine, slot_low, 0.0).astype(BF16), places)
    wanted = (high * 256.0 + low).astype(jnp.int32) - 1
    line = wanted & (rows - 1)
    group = wanted >> shift
    for d in range(devices):
        req_ref[d, :, :cap] = line[d : d + 1]
        req_ref[d, :, cap:] = group[d : d + 1]
    pl.semaphore_wait(barrier, devices - 1)

    @pl.loop(1, devices)
    def _(k):
        push(peer(k), req_ref, asked_ref, 0).start()

    asked_ref[me] = req_ref[me]
    load.wait()
    wide_ref[...] = jnp.zeros_like(wide_ref)
    block = wide_ref.shape[1]

    @pl.loop(0, rows // block)
    def _(j):
        for k in range(8):
            at = pl.ds(pl.multiple_of(k * rows + j * block, block), block)
            wide_ref[k * 16 : k * 16 + CH, :] = params_ref[:, at]
        table_ref[pl.ds(pl.multiple_of(j * block, block), block), :] = jnp.transpose(wide_ref[...])

    drain(req_ref, asked_ref, 0)
    move = pltpu.make_async_copy(asked_ref, lines_ref, local_sem.at[1])
    move.start()
    move.wait()

    eye = jnp.where(iota((128, 128), 0) == iota((128, 128), 1), 1.0, 0.0).astype(BF16)

    def fetch(k, held):
        source = peer(k)
        for j in range(cap):
            held[j : j + 1, :] = table_ref[pl.ds(lines_ref[source, 0, j], 1), :]

    def pick(k, held):
        source = peer(k)
        high, low = split(held[...])
        turned = mm_nt(eye, high) + mm_nt(eye, low)
        group = asked_ref[source, :, cap:]
        found = jnp.zeros((16, cap), F32)
        for q in range(8):
            found = found + jnp.where(group == q, turned[q * 16 : q * 16 + 16], 0.0)
        return found[:CH]

    def answer(k, held):
        source = peer(k)
        found_ref[source] = pick(k, held)
        push(source, found_ref, replies_ref, 1).start()

    fetch(1, even_ref)

    @pl.loop(0, devices // 2 - 1)
    def _(p):
        fetch(2 * p + 2, odd_ref)
        answer(2 * p + 1, even_ref)
        fetch(2 * p + 3, even_ref)
        answer(2 * p + 2, odd_ref)

    answer(devices - 1, even_ref)
    fetch(0, odd_ref)
    replies_ref[me] = pick(0, odd_ref)
    drain(found_ref, replies_ref, 1)

    for ch in range(CH):
        part = slice(ch * devices, (ch + 1) * devices)
        reply_high[part, :], reply_low[part, :] = split(replies_ref[:, ch, :])
    sent_ref[...] = jnp.zeros_like(sent_ref)
    blocks = slots // SB
    centres = iota((SIDE, SB), 0).astype(F32) + 0.5
    side_rows = pixels // SIDE

    @pl.loop(0, tiles)
    def _(tile):
        length = length_ref[tile]
        mine = iota((devices, slots), 0) == live_ref[tile]
        places = one_hot(rank_ref[tile], cap)
        fetched = mm(reply_high[...], places) + mm(reply_low[...], places)
        vals[...] = jnp.zeros_like(vals)
        live = jnp.where(iota((1, slots), 1) < length, 1.0, 0.0)
        for ch in range(CH):
            part = slice(ch * devices, (ch + 1) * devices)
            value = jnp.sum(jnp.where(mine, fetched[part], 0.0), axis=0, keepdims=True)
            if ch == 5:
                value = value * live
            row = ch if ch < 6 else ch + 2
            vals[row : row + 1, :] = value

        carry = jnp.zeros((pixels, 1), F32)
        image = jnp.zeros((pixels, 8), F32)
        for blk in range(blocks):
            at = slice(blk * SB, (blk + 1) * SB)
            dx = centres - vals[0:1, at]
            dy = centres - vals[1:2, at]
            ex = 0.5 * vals[2:3, at] * dx * dx
            ey = 0.5 * vals[4:5, at] * dy * dy
            bdy = vals[3:4, at] * dy
            opacity = vals[5:6, at]
            for y in range(side_rows):
                rows = slice(y * SIDE, (y + 1) * SIDE)
                exponent = ex + ey[y : y + 1] + dx * bdy[y : y + 1]
                falloff = jnp.exp(-exponent)
                falloff_ref[rows, at] = falloff
                keep = jnp.log(1.0 - opacity * falloff)
                high, low = split(keep)
                high_ref[rows, :] = high
                low_ref[rows, :] = low
            total = mm(high_ref[...], strict) + mm(low_ref[...], strict) + carry
            last = high_ref[:, SB - 128 :].astype(F32) + low_ref[:, SB - 128 :].astype(F32)
            carry = total[:, SB - 1 : SB] + last[:, 127:128]
            trans = jnp.exp(total)
            trans_ref[:, at] = trans
            weight_high, weight_low = split(trans * (opacity * falloff_ref[:, at]))
            colour_high, colour_low = split(vals[8:16, at])
            image = image + (
                mm_nt(weight_high, colour_high)
                + mm_nt(weight_high, colour_low)
                + mm_nt(weight_low, colour_high)
            )
        rendered = jnp.transpose(image)
        for ch in range(4):
            image_ref[ch, pl.ds(tile, 1), :] = rendered[ch : ch + 1]
        wished = [target_ref[ch, pl.ds(tile, 1), :] for ch in range(4)]
        wished = jnp.concatenate(wished + [jnp.zeros((4, pixels), F32)], axis=0)
        grad_image = 2.0 * (rendered - wished)
        grad_high, grad_low = split(grad_image)
        grad_wide = grad_high.astype(F32)
        grad_rest = grad_image - grad_wide
        turned = jnp.transpose(jnp.concatenate([grad_wide, grad_wide, grad_rest, grad_image], axis=0))
        turned_parts = turned.astype(BF16)
        grand_total = jnp.sum(jnp.transpose(grad_image) * image, axis=1, keepdims=True)

        spent = jnp.zeros((pixels, 1), F32)
        for blk in range(blocks):
            at = slice(blk * SB, (blk + 1) * SB)
            mean_x, mean_y = vals[0:1, at], vals[1:2, at]
            conic_a, conic_b, conic_c = vals[2:3, at], vals[3:4, at], vals[4:5, at]
            opacity = vals[5:6, at]
            dx = centres - mean_x
            dy = centres - mean_y
            colours = vals[8:16, at]
            colour_wide = colours.astype(BF16).astype(F32)
            colour_parts = jnp.concatenate(
                [colour_wide, colours - colour_wide, colour_wide, jnp.zeros_like(colours)], axis=0
            ).astype(BF16)
            shading = mm(turned_parts, colour_parts)
            shade_ref[...] = shading
            weight = trans_ref[:, at] * (opacity * falloff_ref[:, at])
            weight_high, weight_low = split(weight)
            grads[8:16, at] = (
                mm(grad_high, weight_high) + mm(grad_low, weight_high) + mm(grad_high, weight_low)
            )
            high, low = split(weight * shading)
            before = mm(high, inclusive) + mm(low, inclusive) + spent
            spent = before[:, SB - 1 : SB]
            before_ref[...] = grand_total - before
            power0 = jnp.zeros((SIDE, SB), F32)
            power1 = power0
            power2 = power0
            opaque = power0
            for y in range(side_rows):
                rows = slice(y * SIDE, (y + 1) * SIDE)
                falloff = falloff_ref[rows, at]
                alpha = opacity * falloff
                grad_alpha = trans_ref[rows, at] * shade_ref[rows, :] - before_ref[rows, :] / (
                    1.0 - alpha
                )
                opaque = opaque + grad_alpha * falloff
                power = grad_alpha * alpha
                power0 = power0 - power
                moment = power * dy[y : y + 1]
                power1 = power1 - moment
                power2 = power2 - moment * dy[y : y + 1]
            across = power0 * dx
            sum_x = jnp.sum(across, axis=0, keepdims=True)
            sum_y = jnp.sum(power1, axis=0, keepdims=True)
            grads[0:1, at] = -(conic_a * sum_x + conic_b * sum_y)
            grads[1:2, at] = -(conic_c * sum_y + conic_b * sum_x)
            grads[2:3, at] = 0.5 * jnp.sum(across * dx, axis=0, keepdims=True)
            grads[3:4, at] = jnp.sum(power1 * dx, axis=0, keepdims=True)
            grads[4:5, at] = 0.5 * jnp.sum(power2, axis=0, keepdims=True)
            grads[5:6, at] = jnp.sum(opaque, axis=0, keepdims=True) * live[:, at]

        for ch in range(CH):
            part = slice(ch * devices, (ch + 1) * devices)
            row = ch if ch < 6 else ch + 2
            high, low = split(jnp.where(mine, grads[row : row + 1, :], 0.0))
            pack_ref[0, part, :] = high
            pack_ref[1, part, :] = low
        sent = mm_nt(pack_ref[0], places) + mm_nt(pack_ref[1], places)

        sent_ref[...] += sent

    for ch in range(CH):
        part = slice(ch * devices, (ch + 1) * devices)
        outgoing_ref[:, ch, :] = sent_ref[part, :]

    @pl.loop(1, devices)
    def _(k):
        push(peer(k), outgoing_ref, incoming_ref, 2).start()

    incoming_ref[me] = outgoing_ref[me]
    drain(outgoing_ref, incoming_ref, 2)


def scatter_kernel(row_ref, count_ref, ask_ref, grad_ref, out_ref, wide_ref, *banks):
    rows = banks[0].shape[0]
    devices, _, cap = grad_ref.shape
    width = ask_ref.shape[1]
    steps = ask_ref.shape[0]
    unit = 256

    def clear(j, _):
        at = pl.ds(pl.multiple_of(j * unit, unit), unit)
        for bank in banks:
            bank[at, :] = jnp.zeros((unit, 128), F32)
        return 0

    lax.fori_loop(0, rows // unit, clear, 0)

    def widen(step, _):
        group = ask_ref[pl.ds(step, 1), :]
        parts = [grad_ref[step * (width // cap) + k] for k in range(width // cap)]
        grad = jnp.concatenate(parts, axis=1) if len(parts) > 1 else parts[0]
        grad = jnp.concatenate([grad, jnp.zeros((16 - CH, width), F32)], axis=0)
        wide = jnp.concatenate([jnp.where(group == k, grad, 0.0) for k in range(8)], axis=0)
        wide_ref[pl.ds(pl.multiple_of(step * width, width), width), :] = jnp.transpose(wide)
        return 0

    lax.fori_loop(0, steps, widen, 0)
    burst = 16

    def source(s, _):
        def add(j, _):
            base = s * cap + j * burst
            lines = wide_ref[pl.ds(pl.multiple_of(base, burst), burst), :]
            for u in range(burst):
                bank = banks[u % len(banks)]
                at = pl.ds(row_ref[base + u], 1)
                bank[at, :] = bank[at, :] + lines[u : u + 1]
            return 0

        return lax.fori_loop(0, (count_ref[s] + burst - 1) // burst, add, 0)

    lax.fori_loop(0, devices, source, 0)
    block = 512

    def finish(j, _):
        at = pl.ds(pl.multiple_of(j * block, block), block)
        total = banks[0][at, :]
        for bank in banks[1:]:
            total = total + bank[at, :]
        turned = jnp.transpose(total)
        for k in range(8):
            to = pl.ds(pl.multiple_of(k * rows + j * block, block), block)
            out_ref[:, to] = turned[k * 16 : k * 16 + CH]
        return 0

    lax.fori_loop(0, rows // block, finish, 0)


def body(splat_params, list_owner, list_slot, list_length, target):
    devices = lax.axis_size(("row", "col"))
    tiles, slots = list_slot.shape
    entries = tiles * slots
    splats = splat_params.shape[1]
    pixels = target.shape[2]
    cap = 2 * entries // devices
    total = devices * cap
    rows = splats // 8
    smem = pl.BlockSpec(memory_space=pltpu.SMEM)
    vmem = pl.BlockSpec(memory_space=pltpu.VMEM)
    rendered, asked, incoming = pl.pallas_call(
        step_kernel,
        in_specs=[smem, vmem, vmem, vmem, pl.BlockSpec(memory_space=pl.ANY)],
        out_specs=(vmem, vmem, vmem),
        out_shape=(
            jax.ShapeDtypeStruct((4, tiles, pixels), F32),
            jax.ShapeDtypeStruct((devices, 1, 2 * cap), jnp.int32),
            jax.ShapeDtypeStruct((devices, CH, cap), F32),
        ),
        scratch_shapes=[
            pltpu.VMEM((CH, splats), F32),
            pltpu.VMEM((rows, 128), F32),
            pltpu.VMEM((128, 512), F32),
            pltpu.VMEM((cap, 128), F32),
            pltpu.VMEM((cap, 128), F32),
            pltpu.SMEM((devices, 1, 2 * cap), jnp.int32),
            pltpu.VMEM((tiles, 1, slots), jnp.int32),
            pltpu.VMEM((tiles, 1, slots), jnp.int32),
            pltpu.VMEM((devices, 1, 2 * cap), jnp.int32),
            pltpu.VMEM((devices, CH, cap), F32),
            pltpu.VMEM((devices, CH, cap), F32),
            pltpu.VMEM((devices, CH, cap), F32),
            pltpu.VMEM((CH * devices, cap), BF16),
            pltpu.VMEM((CH * devices, cap), BF16),
            pltpu.VMEM((CH * devices, cap), F32),
            pltpu.VMEM((16, slots), F32),
            pltpu.VMEM((16, slots), F32),
            pltpu.VMEM((pixels, slots), F32),
            pltpu.VMEM((pixels, slots), F32),
            pltpu.VMEM((pixels, SB), BF16),
            pltpu.VMEM((pixels, SB), BF16),
            pltpu.VMEM((pixels, SB), F32),
            pltpu.VMEM((pixels, SB), F32),
            pltpu.VMEM((2, CH * devices, slots), BF16),
            pltpu.SemaphoreType.DMA((2,)),
            pltpu.SemaphoreType.DMA((3,)),
            pltpu.SemaphoreType.DMA((3,)),
        ],
        compiler_params=pltpu.CompilerParams(collective_id=0, has_side_effects=True),
        name="step",
    )(list_length, list_owner.reshape(tiles, 1, slots), list_slot, target, splat_params)
    lines = asked[:, 0, :cap].reshape(total)
    groups = asked[:, 0, cap:]
    counts = jnp.sum((groups >= 0).astype(jnp.int32), axis=1)
    splat_grads = pl.pallas_call(
        scatter_kernel,
        in_specs=[smem, smem, vmem, vmem],
        out_shape=jax.ShapeDtypeStruct((CH, splats), F32),
        scratch_shapes=[pltpu.VMEM((total, 128), F32)] + [pltpu.VMEM((rows, 128), F32)] * 4,
        name="accumulate",
    )(lines, counts, groups.reshape(total // LANES, LANES), incoming)
    return (rendered, splat_grads)


def solution(mesh):
    in_specs = (
        P(None, ("row", "col")),
        P(("row", "col"), None, None),
        P(("row", "col"), None),
        P(("row", "col")),
        P(None, ("row", "col"), None),
    )
    out_specs = (P(None, ("row", "col"), None), P(None, ("row", "col")))
    return jax.shard_map(body, mesh=mesh, in_specs=in_specs, out_specs=out_specs, check_vma=False)
```

```python
import functools

import jax
import jax.numpy as jnp
from jax import lax
from jax.experimental import pallas as pl
from jax.experimental.pallas import tpu as pltpu
from jax.sharding import PartitionSpec as P

SIDE = 16
SB = 256
CH = 10
F32 = jnp.float32
BF16 = jnp.bfloat16
NT = (((1,), (1,)), ((), ()))
BLOCK = 512


def iota(shape, dim):
    return lax.broadcasted_iota(jnp.int32, shape, dim)


def split(x):
    high = x.astype(BF16)
    return high, (x - high.astype(F32)).astype(BF16)


def mm(a, b):
    return jnp.dot(a, b, preferred_element_type=F32)


def mm_nt(a, b):
    return lax.dot_general(a, b, NT, preferred_element_type=F32)


def one_hot(index, size):
    return jnp.where(iota((size, index.shape[1]), 0) == index, 1.0, 0.0).astype(BF16)


def step_kernel(
    length_ref, own_ref, slot_ref, target_ref, params_hbm, image_ref, asked_ref, incoming_ref, coming_ref,
    params_ref, table_ref, wide_ref, even_ref, odd_ref, lines_ref, live_ref, rank_ref, req_ref,
    found_ref, find_ref, replies_ref, reply_ref, outgoing_ref, going_ref, reply_high, reply_low, sent_ref,
    vals, grads, falloff_ref, trans_ref, high_ref, low_ref, shade_ref, before_ref, pack_ref,
    local_sem, send_sem, recv_sem,
):
    rows_on = lax.axis_size("row")
    cols_on = lax.axis_size("col")
    devices = rows_on * cols_on
    me = lax.axis_index("row") * cols_on + lax.axis_index("col")
    tiles, slots = slot_ref.shape
    cap = found_ref.shape[2]
    pixels = target_ref.shape[2]
    rows = table_ref.shape[0]
    others = pl.ds(0, devices - 1)

    def peer(k):
        return lax.rem(me + k, devices)

    def place_of(device):
        return (device // cols_on, lax.rem(device, cols_on))

    def push(device, source, target, phase):
        return pltpu.make_async_remote_copy(
            src_ref=source.at[device],
            dst_ref=target.at[me],
            send_sem=send_sem.at[phase],
            recv_sem=recv_sem.at[phase],
            device_id=place_of(device),
            device_id_type=pl.DeviceIdType.MESH,
        )

    def drain(source, target, phase):
        pltpu.make_async_copy(target.at[others], target.at[others], recv_sem.at[phase]).wait()
        pltpu.make_async_copy(source.at[others], source.at[others], send_sem.at[phase]).wait()

    barrier = pltpu.get_barrier_semaphore()

    @pl.loop(1, devices)
    def _(k):
        pl.semaphore_signal(
            barrier, inc=1, device_id=place_of(peer(k)), device_id_type=pl.DeviceIdType.MESH
        )

    load = pltpu.make_async_copy(params_hbm, params_ref, local_sem.at[0])
    load.start()

    strict = jnp.where(iota((SB, SB), 0) < iota((SB, SB), 1), 1.0, 0.0).astype(BF16)
    inclusive = jnp.where(iota((SB, SB), 0) <= iota((SB, SB), 1), 1.0, 0.0).astype(BF16)
    count = jnp.zeros((devices, 1), F32)
    high = jnp.zeros((devices, cap), F32)
    low = jnp.zeros((devices, cap), F32)
    for tile in range(tiles):
        for j in range(slots // SB):
            part = slice(j * SB, (j + 1) * SB)
            owner = jnp.where(iota((1, SB), 1) + j * SB < length_ref[tile], own_ref[tile, :, part], -1)
            live_ref[tile, :, part] = owner
            mine = iota((devices, SB), 0) == owner
            ones = jnp.where(mine, 1.0, 0.0)
            ahead = mm(ones.astype(BF16), strict) + count
            rank = jnp.sum(ones * ahead, axis=0, keepdims=True).astype(jnp.int32)
            count = count + jnp.sum(ones, axis=1, keepdims=True)
            rank_ref[tile, :, part] = rank
            named = slot_ref[tile : tile + 1, part]
            places = one_hot(rank, cap)
            slot_high = (named >> 8).astype(F32)
            slot_low = ((named & 255) + 1).astype(F32)
            high = high + mm_nt(jnp.where(mine, slot_high, 0.0).astype(BF16), places)
            low = low + mm_nt(jnp.where(mine, slot_low, 0.0).astype(BF16), places)
    wanted = (high * 256.0 + low).astype(jnp.int32) - 1
    chunk = wanted >> (8 * BLOCK).bit_length() - 1
    line = (chunk & (rows // BLOCK - 1)) * BLOCK + (wanted & (BLOCK - 1))
    group = jnp.where(wanted < 0, -1, (wanted >> BLOCK.bit_length() - 1) & 7)
    filled = jnp.broadcast_to(count, (devices, 128)).astype(jnp.int32)
    for d in range(devices):
        req_ref[d, :, :cap] = line[d : d + 1]
        req_ref[d, :, cap : 2 * cap] = group[d : d + 1]
        req_ref[d, :, 2 * cap :] = filled[d : d + 1]
    pl.semaphore_wait(barrier, devices - 1)

    @pl.loop(1, devices)
    def _(k):
        push(peer(k), req_ref, asked_ref, 0).start()

    asked_ref[me] = req_ref[me]
    load.wait()
    wide_ref[...] = jnp.zeros_like(wide_ref)

    @pl.loop(0, rows // BLOCK)
    def _(j):
        for k in range(8):
            at = pl.ds(pl.multiple_of((j * 8 + k) * BLOCK, BLOCK), BLOCK)
            wide_ref[k * 16 : k * 16 + CH, :] = params_ref[:, at]
        table_ref[pl.ds(pl.multiple_of(j * BLOCK, BLOCK), BLOCK), :] = jnp.transpose(wide_ref[...])

    drain(req_ref, asked_ref, 0)
    move = pltpu.make_async_copy(asked_ref, lines_ref, local_sem.at[1])
    move.start()
    move.wait()

    eye = jnp.where(iota((128, 128), 0) == iota((128, 128), 1), 1.0, 0.0).astype(BF16)

    def fetch(k, held):
        source = peer(k)
        for j in range(cap):
            held[j : j + 1, :] = table_ref[pl.ds(lines_ref[source, 0, j], 1), :]

    def pick(k, held):
        source = peer(k)
        high, low = split(held[...])
        turned = mm_nt(eye, high) + mm_nt(eye, low)
        group = asked_ref[source, :, cap : 2 * cap]
        found = jnp.zeros((16, cap), F32)
        for q in range(8):
            found = found + jnp.where(group == q, turned[q * 16 : q * 16 + 16], 0.0)
        return found[:8], found[8:CH]

    def answer(k, held):
        source = peer(k)
        found_ref[source], find_ref[source] = pick(k, held)
        push(source, found_ref, replies_ref, 1).start()
        push(source, find_ref, reply_ref, 2).start()

    fetch(1, even_ref)

    @pl.loop(0, devices // 2 - 1)
    def _(p):
        fetch(2 * p + 2, odd_ref)
        answer(2 * p + 1, even_ref)
        fetch(2 * p + 3, even_ref)
        answer(2 * p + 2, odd_ref)

    answer(devices - 1, even_ref)
    fetch(0, odd_ref)
    replies_ref[me], reply_ref[me] = pick(0, odd_ref)
    drain(found_ref, replies_ref, 1)
    drain(find_ref, reply_ref, 2)

    for ch in range(CH):
        part = slice(ch * devices, (ch + 1) * devices)
        reply_high[part, :], reply_low[part, :] = split(replies_ref[:, ch, :] if ch < 8 else reply_ref[:, ch - 8, :])
    sent_ref[...] = jnp.zeros_like(sent_ref)
    blocks = slots // SB
    centres = iota((SIDE, SB), 0).astype(F32) + 0.5
    side_rows = pixels // SIDE

    @pl.loop(0, tiles)
    def _(tile):
        length = length_ref[tile]
        mine = iota((devices, slots), 0) == live_ref[tile]
        places = one_hot(rank_ref[tile], cap)
        fetched = mm(reply_high[...], places) + mm(reply_low[...], places)
        vals[...] = jnp.zeros_like(vals)
        live = jnp.where(iota((1, slots), 1) < length, 1.0, 0.0)
        for ch in range(CH):
            part = slice(ch * devices, (ch + 1) * devices)
            value = jnp.sum(jnp.where(mine, fetched[part], 0.0), axis=0, keepdims=True)
            if ch == 5:
                value = value * live
            row = ch if ch < 6 else ch + 2
            vals[row : row + 1, :] = value

        carry = jnp.zeros((pixels, 1), F32)
        image = jnp.zeros((pixels, 8), F32)
        for blk in range(blocks):
            at = slice(blk * SB, (blk + 1) * SB)
            dx = centres - vals[0:1, at]
            dy = centres - vals[1:2, at]
            ex = 0.5 * vals[2:3, at] * dx * dx
            ey = 0.5 * vals[4:5, at] * dy * dy
            bdy = vals[3:4, at] * dy
            opacity = vals[5:6, at]
            for y in range(side_rows):
                rows = slice(y * SIDE, (y + 1) * SIDE)
                exponent = ex + ey[y : y + 1] + dx * bdy[y : y + 1]
                falloff = jnp.exp(-exponent)
                falloff_ref[rows, at] = falloff
                keep = jnp.log(1.0 - opacity * falloff)
                high, low = split(keep)
                high_ref[rows, :] = high
                low_ref[rows, :] = low
            total = mm(high_ref[...], strict) + mm(low_ref[...], strict) + carry
            last = high_ref[:, SB - 128 :].astype(F32) + low_ref[:, SB - 128 :].astype(F32)
            carry = total[:, SB - 1 : SB] + last[:, 127:128]
            trans = jnp.exp(total)
            trans_ref[:, at] = trans
            weight_high, weight_low = split(trans * (opacity * falloff_ref[:, at]))
            colour_high, colour_low = split(vals[8:16, at])
            image = image + (
                mm_nt(weight_high, colour_high)
                + mm_nt(weight_high, colour_low)
                + mm_nt(weight_low, colour_high)
            )
        rendered = jnp.transpose(image)
        for ch in range(4):
            image_ref[ch, pl.ds(tile, 1), :] = rendered[ch : ch + 1]
        wished = [target_ref[ch, pl.ds(tile, 1), :] for ch in range(4)]
        wished = jnp.concatenate(wished + [jnp.zeros((4, pixels), F32)], axis=0)
        grad_image = 2.0 * (rendered - wished)
        grad_high, grad_low = split(grad_image)
        grad_wide = grad_high.astype(F32)
        grad_rest = grad_image - grad_wide
        turned = jnp.transpose(jnp.concatenate([grad_wide, grad_wide, grad_rest, grad_image], axis=0))
        turned_parts = turned.astype(BF16)
        grand_total = jnp.sum(jnp.transpose(grad_image) * image, axis=1, keepdims=True)

        spent = jnp.zeros((pixels, 1), F32)
        for blk in range(blocks):
            at = slice(blk * SB, (blk + 1) * SB)
            mean_x, mean_y = vals[0:1, at], vals[1:2, at]
            conic_a, conic_b, conic_c = vals[2:3, at], vals[3:4, at], vals[4:5, at]
            opacity = vals[5:6, at]
            dx = centres - mean_x
            dy = centres - mean_y
            colours = vals[8:16, at]
            colour_wide = colours.astype(BF16).astype(F32)
            colour_parts = jnp.concatenate(
                [colour_wide, colours - colour_wide, colour_wide, jnp.zeros_like(colours)], axis=0
            ).astype(BF16)
            shading = mm(turned_parts, colour_parts)
            shade_ref[...] = shading
            weight = trans_ref[:, at] * (opacity * falloff_ref[:, at])
            weight_high, weight_low = split(weight)
            grads[8:16, at] = (
                mm(grad_high, weight_high) + mm(grad_low, weight_high) + mm(grad_high, weight_low)
            )
            high, low = split(weight * shading)
            before = mm(high, inclusive) + mm(low, inclusive) + spent
            spent = before[:, SB - 1 : SB]
            before_ref[...] = grand_total - before
            power0 = jnp.zeros((SIDE, SB), F32)
            power1 = power0
            power2 = power0
            opaque = power0
            for y in range(side_rows):
                rows = slice(y * SIDE, (y + 1) * SIDE)
                falloff = falloff_ref[rows, at]
                alpha = opacity * falloff
                grad_alpha = trans_ref[rows, at] * shade_ref[rows, :] - before_ref[rows, :] / (
                    1.0 - alpha
                )
                opaque = opaque + grad_alpha * falloff
                power = grad_alpha * alpha
                power0 = power0 - power
                moment = power * dy[y : y + 1]
                power1 = power1 - moment
                power2 = power2 - moment * dy[y : y + 1]
            across = power0 * dx
            sum_x = jnp.sum(across, axis=0, keepdims=True)
            sum_y = jnp.sum(power1, axis=0, keepdims=True)
            grads[0:1, at] = -(conic_a * sum_x + conic_b * sum_y)
            grads[1:2, at] = -(conic_c * sum_y + conic_b * sum_x)
            grads[2:3, at] = 0.5 * jnp.sum(across * dx, axis=0, keepdims=True)
            grads[3:4, at] = jnp.sum(power1 * dx, axis=0, keepdims=True)
            grads[4:5, at] = 0.5 * jnp.sum(power2, axis=0, keepdims=True)
            grads[5:6, at] = jnp.sum(opaque, axis=0, keepdims=True) * live[:, at]

        for ch in range(CH):
            part = slice(ch * devices, (ch + 1) * devices)
            row = ch if ch < 6 else ch + 2
            high, low = split(jnp.where(mine, grads[row : row + 1, :], 0.0))
            pack_ref[0, part, :] = high
            pack_ref[1, part, :] = low
        sent = mm_nt(pack_ref[0], places) + mm_nt(pack_ref[1], places)

        sent_ref[...] += sent

    for ch in range(CH):
        part = slice(ch * devices, (ch + 1) * devices)
        if ch < 8:
            outgoing_ref[:, ch, :] = sent_ref[part, :]
        else:
            going_ref[:, ch - 8, :] = sent_ref[part, :]

    @pl.loop(1, devices)
    def _(k):
        push(peer(k), outgoing_ref, incoming_ref, 3).start()
        push(peer(k), going_ref, coming_ref, 4).start()

    incoming_ref[me] = outgoing_ref[me]
    coming_ref[me] = going_ref[me]
    drain(outgoing_ref, incoming_ref, 3)
    drain(going_ref, coming_ref, 4)


def scatter_kernel(
    line_ref, ask_ref, grad_ref, rest_ref, out_hbm, wide_ref, out_ref, out_sem, *banks
):
    rows = banks[0].shape[0]
    devices, _, cap = grad_ref.shape
    share = rows // devices
    burst = 32

    @pl.loop(0, devices)
    def _(s):
        at = pl.ds(pl.multiple_of(s * share, share), share)
        for bank in banks:
            bank[at, :] = jnp.zeros((share, 128), F32)
        group = ask_ref[s, :, cap : 2 * cap]
        grad = jnp.concatenate([grad_ref[s], rest_ref[s], jnp.zeros((16 - CH, cap), F32)], axis=0)
        wide = jnp.concatenate([jnp.where(group == k, grad, 0.0) for k in range(8)], axis=0)
        wide_ref[pl.ds(pl.multiple_of(s * cap, cap), cap), :] = jnp.transpose(wide)

    @pl.loop(0, devices)
    def _(s):
        @pl.loop(0, (line_ref[s, 0, 2 * cap] + burst - 1) // burst)
        def _(j):
            first = j * burst
            lines = wide_ref[pl.ds(pl.multiple_of(s * cap + first, burst), burst), :]
            for u in range(burst):
                bank = banks[u % len(banks)]
                at = pl.ds(line_ref[s, 0, first + u], 1)
                bank[at, :] = bank[at, :] + lines[u : u + 1]

    def leave(j):
        to = pl.ds(pl.multiple_of(j * 8 * BLOCK, 8 * BLOCK), 8 * BLOCK)
        return pltpu.make_async_copy(out_ref.at[:, to], out_hbm.at[:, to], out_sem)

    @pl.loop(0, rows // BLOCK)
    def _(j):
        at = pl.ds(pl.multiple_of(j * BLOCK, BLOCK), BLOCK)
        total = banks[0][at, :]
        for bank in banks[1:]:
            total = total + bank[at, :]
        turned = jnp.transpose(total)
        for k in range(8):
            to = pl.ds(pl.multiple_of((j * 8 + k) * BLOCK, BLOCK), BLOCK)
            out_ref[:, to] = turned[k * 16 : k * 16 + CH]
        leave(j).start()

    pltpu.make_async_copy(out_ref, out_hbm, out_sem).wait()


def body(splat_params, list_owner, list_slot, list_length, target):
    devices = lax.axis_size(("row", "col"))
    tiles, slots = list_slot.shape
    entries = tiles * slots
    splats = splat_params.shape[1]
    pixels = target.shape[2]
    cap = 2 * entries // devices
    total = devices * cap
    rows = splats // 8
    smem = pl.BlockSpec(memory_space=pltpu.SMEM)
    vmem = pl.BlockSpec(memory_space=pltpu.VMEM)
    rendered, asked, incoming, coming = pl.pallas_call(
        step_kernel,
        in_specs=[smem, vmem, vmem, vmem, pl.BlockSpec(memory_space=pl.ANY)],
        out_specs=(vmem, vmem, vmem, vmem),
        out_shape=(
            jax.ShapeDtypeStruct((4, tiles, pixels), F32),
            jax.ShapeDtypeStruct((devices, 1, 2 * cap + 128), jnp.int32),
            jax.ShapeDtypeStruct((devices, 8, cap), F32),
            jax.ShapeDtypeStruct((devices, CH - 8, cap), F32),
        ),
        scratch_shapes=[
            pltpu.VMEM((CH, splats), F32),
            pltpu.VMEM((rows, 128), F32),
            pltpu.VMEM((128, BLOCK), F32),
            pltpu.VMEM((cap, 128), F32),
            pltpu.VMEM((cap, 128), F32),
            pltpu.SMEM((devices, 1, 2 * cap + 128), jnp.int32),
            pltpu.VMEM((tiles, 1, slots), jnp.int32),
            pltpu.VMEM((tiles, 1, slots), jnp.int32),
            pltpu.VMEM((devices, 1, 2 * cap + 128), jnp.int32),
            pltpu.VMEM((devices, 8, cap), F32),
            pltpu.VMEM((devices, CH - 8, cap), F32),
            pltpu.VMEM((devices, 8, cap), F32),
            pltpu.VMEM((devices, CH - 8, cap), F32),
            pltpu.VMEM((devices, 8, cap), F32),
            pltpu.VMEM((devices, CH - 8, cap), F32),
            pltpu.VMEM((CH * devices, cap), BF16),
            pltpu.VMEM((CH * devices, cap), BF16),
            pltpu.VMEM((CH * devices, cap), F32),
            pltpu.VMEM((16, slots), F32),
            pltpu.VMEM((16, slots), F32),
            pltpu.VMEM((pixels, slots), F32),
            pltpu.VMEM((pixels, slots), F32),
            pltpu.VMEM((pixels, SB), BF16),
            pltpu.VMEM((pixels, SB), BF16),
            pltpu.VMEM((pixels, SB), F32),
            pltpu.VMEM((pixels, SB), F32),
            pltpu.VMEM((2, CH * devices, slots), BF16),
            pltpu.SemaphoreType.DMA((2,)),
            pltpu.SemaphoreType.DMA((5,)),
            pltpu.SemaphoreType.DMA((5,)),
        ],
        compiler_params=pltpu.CompilerParams(collective_id=0, has_side_effects=True),
        name="step",
    )(list_length, list_owner.reshape(tiles, 1, slots), list_slot, target, splat_params)
    splat_grads = pl.pallas_call(
        scatter_kernel,
        in_specs=[smem, vmem, vmem, vmem],
        out_specs=pl.BlockSpec(memory_space=pl.ANY),
        out_shape=jax.ShapeDtypeStruct((CH, splats), F32),
        scratch_shapes=[
            pltpu.VMEM((total, 128), F32),
            pltpu.VMEM((CH, splats), F32),
            pltpu.SemaphoreType.DMA,
        ]
        + [pltpu.VMEM((rows, 128), F32)] * 4,
        name="accumulate",
    )(asked, asked, incoming, coming)
    return (rendered, splat_grads)


def solution(mesh):
    in_specs = (
        P(None, ("row", "col")),
        P(("row", "col"), None, None),
        P(("row", "col"), None),
        P(("row", "col")),
        P(None, ("row", "col"), None),
    )
    out_specs = (P(None, ("row", "col"), None), P(None, ("row", "col")))
    return jax.shard_map(body, mesh=mesh, in_specs=in_specs, out_specs=out_specs, check_vma=False)
```

```python
import functools

import jax
import jax.numpy as jnp
from jax import lax
from jax.experimental import pallas as pl
from jax.experimental.pallas import tpu as pltpu
from jax.sharding import PartitionSpec as P

SIDE = 16
SB = 256
CH = 10
F32 = jnp.float32
BF16 = jnp.bfloat16
NT = (((1,), (1,)), ((), ()))
BLOCK = 512
LOG2E = 1.4426950408889634


def iota(shape, dim):
    return lax.broadcasted_iota(jnp.int32, shape, dim)


def split(x):
    high = x.astype(BF16)
    return high, (x - high.astype(F32)).astype(BF16)


def mm(a, b):
    return jnp.dot(a, b, preferred_element_type=F32)


def mm_nt(a, b):
    return lax.dot_general(a, b, NT, preferred_element_type=F32)


def one_hot(index, size):
    return jnp.where(iota((size, index.shape[1]), 0) == index, 1.0, 0.0).astype(BF16)


def step_kernel(
    length_ref, own_ref, slot_ref, target_ref, params_hbm, image_ref, asked_ref, incoming_ref, coming_ref,
    params_ref, table_ref, wide_ref, even_ref, odd_ref, lines_ref, live_ref, rank_ref, req_ref,
    found_ref, find_ref, replies_ref, reply_ref, outgoing_ref, going_ref, reply_both, sent_ref,
    vals, grads, falloff_ref, trans_ref, both_ref, shade_ref, after_ref, pack_ref, heavy_ref, light_ref,
    local_sem, send_sem, recv_sem,
):
    rows_on = lax.axis_size("row")
    cols_on = lax.axis_size("col")
    devices = rows_on * cols_on
    me = lax.axis_index("row") * cols_on + lax.axis_index("col")
    tiles, slots = slot_ref.shape
    cap = found_ref.shape[2]
    pixels = target_ref.shape[2]
    rows = table_ref.shape[0]
    others = pl.ds(0, devices - 1)

    def peer(k):
        return lax.rem(me + k, devices)

    def place_of(device):
        return (device // cols_on, lax.rem(device, cols_on))

    def push(device, source, target, phase):
        return pltpu.make_async_remote_copy(
            src_ref=source.at[device],
            dst_ref=target.at[me],
            send_sem=send_sem.at[phase],
            recv_sem=recv_sem.at[phase],
            device_id=place_of(device),
            device_id_type=pl.DeviceIdType.MESH,
        )

    def drain(source, target, phase):
        pltpu.make_async_copy(target.at[others], target.at[others], recv_sem.at[phase]).wait()
        pltpu.make_async_copy(source.at[others], source.at[others], send_sem.at[phase]).wait()

    barrier = pltpu.get_barrier_semaphore()

    @pl.loop(1, devices)
    def _(k):
        pl.semaphore_signal(
            barrier, inc=1, device_id=place_of(peer(k)), device_id_type=pl.DeviceIdType.MESH
        )

    load = pltpu.make_async_copy(params_hbm, params_ref, local_sem.at[0])
    load.start()

    strict = jnp.where(iota((SB, SB), 0) < iota((SB, SB), 1), 1.0, 0.0).astype(BF16)
    later = jnp.where(iota((SB, SB), 0) > iota((SB, SB), 1), 1.0, 0.0).astype(BF16)
    strict_twice = jnp.concatenate([strict, strict], axis=0)
    later_twice = jnp.concatenate([later, later], axis=0)
    count = jnp.zeros((devices, 1), F32)
    high = jnp.zeros((devices, cap), F32)
    low = jnp.zeros((devices, cap), F32)
    for tile in range(tiles):
        for j in range(slots // SB):
            part = slice(j * SB, (j + 1) * SB)
            owner = jnp.where(iota((1, SB), 1) + j * SB < length_ref[tile], own_ref[tile, :, part], -1)
            live_ref[tile, :, part] = owner
            mine = iota((devices, SB), 0) == owner
            ones = jnp.where(mine, 1.0, 0.0)
            ahead = mm(ones.astype(BF16), strict) + count
            rank = jnp.sum(ones * ahead, axis=0, keepdims=True).astype(jnp.int32)
            count = count + jnp.sum(ones, axis=1, keepdims=True)
            rank_ref[tile, :, part] = rank
            named = slot_ref[tile : tile + 1, part]
            places = one_hot(rank, cap)
            slot_high = (named >> 8).astype(F32)
            slot_low = ((named & 255) + 1).astype(F32)
            high = high + mm_nt(jnp.where(mine, slot_high, 0.0).astype(BF16), places)
            low = low + mm_nt(jnp.where(mine, slot_low, 0.0).astype(BF16), places)
    wanted = (high * 256.0 + low).astype(jnp.int32) - 1
    chunk = wanted >> (8 * BLOCK).bit_length() - 1
    line = (chunk & (rows // BLOCK - 1)) * BLOCK + (wanted & (BLOCK - 1))
    group = jnp.where(wanted < 0, -1, (wanted >> BLOCK.bit_length() - 1) & 7)
    filled = jnp.broadcast_to(count, (devices, 128)).astype(jnp.int32)
    for d in range(devices):
        req_ref[d, :, :cap] = line[d : d + 1]
        req_ref[d, :, cap : 2 * cap] = group[d : d + 1]
        req_ref[d, :, 2 * cap :] = filled[d : d + 1]
    pl.semaphore_wait(barrier, devices - 1)

    @pl.loop(1, devices)
    def _(k):
        push(peer(k), req_ref, asked_ref, 0).start()

    asked_ref[me] = req_ref[me]
    load.wait()
    wide_ref[...] = jnp.zeros_like(wide_ref)

    @pl.loop(0, rows // BLOCK)
    def _(j):
        for k in range(8):
            at = pl.ds(pl.multiple_of((j * 8 + k) * BLOCK, BLOCK), BLOCK)
            wide_ref[k * 16 : k * 16 + CH, :] = params_ref[:, at]
        table_ref[pl.ds(pl.multiple_of(j * BLOCK, BLOCK), BLOCK), :] = jnp.transpose(wide_ref[...])

    drain(req_ref, asked_ref, 0)
    move = pltpu.make_async_copy(asked_ref, lines_ref, local_sem.at[1])
    move.start()
    move.wait()

    eye = jnp.where(iota((128, 128), 0) == iota((128, 128), 1), 1.0, 0.0).astype(BF16)

    def fetch(k, held):
        source = peer(k)
        for j in range(cap):
            held[j : j + 1, :] = table_ref[pl.ds(lines_ref[source, 0, j], 1), :]

    def pick(k, held):
        source = peer(k)
        high, low = split(held[...])
        turned = mm_nt(eye, high) + mm_nt(eye, low)
        group = asked_ref[source, :, cap : 2 * cap]
        found = jnp.zeros((16, cap), F32)
        for q in range(8):
            found = found + jnp.where(group == q, turned[q * 16 : q * 16 + 16], 0.0)
        return found[:8], found[8:CH]

    def answer(k, held):
        source = peer(k)
        found_ref[source], find_ref[source] = pick(k, held)
        push(source, found_ref, replies_ref, 1).start()
        push(source, find_ref, reply_ref, 2).start()

    fetch(1, even_ref)

    @pl.loop(0, devices // 2 - 1)
    def _(p):
        fetch(2 * p + 2, odd_ref)
        answer(2 * p + 1, even_ref)
        fetch(2 * p + 3, even_ref)
        answer(2 * p + 2, odd_ref)

    answer(devices - 1, even_ref)
    fetch(0, odd_ref)
    replies_ref[me], reply_ref[me] = pick(0, odd_ref)
    drain(found_ref, replies_ref, 1)
    drain(find_ref, reply_ref, 2)

    for ch in range(CH):
        part = slice(ch * devices, (ch + 1) * devices)
        reply_both[part, :cap], reply_both[part, cap:] = split(replies_ref[:, ch, :] if ch < 8 else reply_ref[:, ch - 8, :])
    sent_ref[...] = jnp.zeros_like(sent_ref)
    blocks = slots // SB
    centres = iota((SIDE, SB), 0).astype(F32) + 0.5
    side_rows = pixels // SIDE

    @pl.loop(0, tiles)
    def _(tile):
        length = length_ref[tile]
        mine = iota((devices, slots), 0) == live_ref[tile]
        places = one_hot(rank_ref[tile], cap)
        fetched = mm(reply_both[...], jnp.concatenate([places, places], axis=0))
        vals[...] = jnp.zeros_like(vals)
        live = jnp.where(iota((1, slots), 1) < length, 1.0, 0.0)
        for ch in range(CH):
            part = slice(ch * devices, (ch + 1) * devices)
            value = jnp.sum(jnp.where(mine, fetched[part], 0.0), axis=0, keepdims=True)
            if ch == 5:
                value = value * live
            row = ch if ch < 6 else ch + 2
            vals[row : row + 1, :] = value

        carry = jnp.zeros((pixels, 1), F32)
        image = jnp.zeros((pixels, 16), F32)
        image_light = jnp.zeros((pixels, 8), F32)
        for blk in range(blocks):
            at = slice(blk * SB, (blk + 1) * SB)
            dx = centres - vals[0:1, at]
            dy = centres - vals[1:2, at]
            ex = (-0.5 * LOG2E) * vals[2:3, at] * dx * dx
            ey = (-0.5 * LOG2E) * vals[4:5, at] * dy * dy
            bdy = -LOG2E * vals[3:4, at] * dy
            opacity = vals[5:6, at]
            for y in range(side_rows):
                rows_at = slice(y * SIDE, (y + 1) * SIDE)
                falloff = jnp.exp2(ex + ey[y : y + 1] + dx * bdy[y : y + 1])
                falloff_ref[rows_at, at] = falloff
                both_ref[rows_at, :SB], both_ref[rows_at, SB:] = split(jnp.log2(1.0 - opacity * falloff))
            total = mm(both_ref[...], strict_twice) + carry
            last = both_ref[:, SB - 128 : SB].astype(F32) + both_ref[:, 2 * SB - 128 :].astype(F32)
            carry = total[:, SB - 1 : SB] + last[:, 127:128]
            trans = jnp.exp2(total)
            trans_ref[:, at] = trans
            weight_high, weight_low = split(trans * (opacity * falloff_ref[:, at]))
            heavy_ref[:, at] = weight_high
            light_ref[:, at] = weight_low
            colour_high, colour_low = split(vals[8:16, at])
            image = image + mm_nt(weight_high, jnp.concatenate([colour_high, colour_low], axis=0))
            image_light = image_light + mm_nt(weight_low, colour_high)
        turned_image = jnp.transpose(image)
        rendered = turned_image[:8] + turned_image[8:] + jnp.transpose(image_light)
        for ch in range(4):
            image_ref[ch, pl.ds(tile, 1), :] = rendered[ch : ch + 1]
        wished = [target_ref[ch, pl.ds(tile, 1), :] for ch in range(4)]
        wished = jnp.concatenate(wished + [jnp.zeros((4, pixels), F32)], axis=0)
        grad_image = 2.0 * (rendered - wished)
        grad_high, grad_low = split(grad_image)
        grad_wide = grad_high.astype(F32)
        grad_rest = grad_image - grad_wide
        turned = jnp.transpose(jnp.concatenate([grad_wide, grad_wide, grad_rest, grad_image], axis=0))
        turned_parts = turned.astype(BF16)
        grad_both = jnp.concatenate([grad_high, grad_low], axis=0)

        spent = jnp.zeros((pixels, 1), F32)
        for blk in reversed(range(blocks)):
            at = slice(blk * SB, (blk + 1) * SB)
            mean_x, mean_y = vals[0:1, at], vals[1:2, at]
            conic_a, conic_b, conic_c = vals[2:3, at], vals[3:4, at], vals[4:5, at]
            opacity = vals[5:6, at]
            dx = centres - mean_x
            dy = centres - mean_y
            colours = vals[8:16, at]
            colour_wide = colours.astype(BF16).astype(F32)
            colour_parts = jnp.concatenate(
                [colour_wide, colours - colour_wide, colour_wide, jnp.zeros_like(colours)], axis=0
            ).astype(BF16)
            shading = mm(turned_parts, colour_parts)
            shade_ref[...] = shading
            colour_grads = mm(grad_both, heavy_ref[:, at])
            grads[8:16, at] = colour_grads[:8] + colour_grads[8:] + mm(grad_high, light_ref[:, at])
            gain = trans_ref[:, at] * (opacity * falloff_ref[:, at]) * shading
            both_ref[:, :SB], both_ref[:, SB:] = split(gain)
            after = mm(both_ref[...], later_twice) + spent
            spent = after[:, 0:1] + gain[:, 0:1]
            after_ref[...] = after
            moment0 = jnp.zeros((SIDE, SB), F32)
            moment1 = moment0
            moment2 = moment0
            for y in range(side_rows):
                rows_at = slice(y * SIDE, (y + 1) * SIDE)
                falloff = falloff_ref[rows_at, at]
                grad_alpha = trans_ref[rows_at, at] * shade_ref[rows_at, :] - after_ref[rows_at, :] / (
                    1.0 - opacity * falloff
                )
                opaque = grad_alpha * falloff
                moment0 = moment0 + opaque
                lever = opaque * dy[y : y + 1]
                moment1 = moment1 + lever
                moment2 = moment2 + lever * dy[y : y + 1]
            across = moment0 * dx
            sum_x = jnp.sum(across, axis=0, keepdims=True)
            sum_y = jnp.sum(moment1, axis=0, keepdims=True)
            grads[0:1, at] = opacity * (conic_a * sum_x + conic_b * sum_y)
            grads[1:2, at] = opacity * (conic_c * sum_y + conic_b * sum_x)
            grads[2:3, at] = -0.5 * opacity * jnp.sum(across * dx, axis=0, keepdims=True)
            grads[3:4, at] = -opacity * jnp.sum(moment1 * dx, axis=0, keepdims=True)
            grads[4:5, at] = -0.5 * opacity * jnp.sum(moment2, axis=0, keepdims=True)
            grads[5:6, at] = jnp.sum(moment0, axis=0, keepdims=True) * live[:, at]

        for ch in range(CH):
            part = slice(ch * devices, (ch + 1) * devices)
            row = ch if ch < 6 else ch + 2
            high, low = split(jnp.where(mine, grads[row : row + 1, :], 0.0))
            pack_ref[part, :slots] = high
            pack_ref[part, slots:] = low
        sent = mm_nt(pack_ref[...], jnp.concatenate([places, places], axis=1))

        sent_ref[...] += sent

    for ch in range(CH):
        part = slice(ch * devices, (ch + 1) * devices)
        if ch < 8:
            outgoing_ref[:, ch, :] = sent_ref[part, :]
        else:
            going_ref[:, ch - 8, :] = sent_ref[part, :]

    @pl.loop(1, devices)
    def _(k):
        push(peer(k), outgoing_ref, incoming_ref, 3).start()
        push(peer(k), going_ref, coming_ref, 4).start()

    incoming_ref[me] = outgoing_ref[me]
    coming_ref[me] = going_ref[me]
    drain(outgoing_ref, incoming_ref, 3)
    drain(going_ref, coming_ref, 4)


def scatter_kernel(
    line_ref, ask_ref, grad_ref, rest_ref, out_hbm, wide_ref, out_ref, out_sem, *banks
):
    rows = banks[0].shape[0]
    devices, _, cap = grad_ref.shape
    share = rows // devices
    burst = 32

    @pl.loop(0, devices)
    def _(s):
        at = pl.ds(pl.multiple_of(s * share, share), share)
        for bank in banks:
            bank[at, :] = jnp.zeros((share, 128), F32)
        group = ask_ref[s, :, cap : 2 * cap]
        grad = jnp.concatenate([grad_ref[s], rest_ref[s], jnp.zeros((16 - CH, cap), F32)], axis=0)
        wide = jnp.concatenate([jnp.where(group == k, grad, 0.0) for k in range(8)], axis=0)
        wide_ref[pl.ds(pl.multiple_of(s * cap, cap), cap), :] = jnp.transpose(wide)

    @pl.loop(0, devices)
    def _(s):
        base = s * (line_ref.shape[0] // devices)

        @pl.loop(0, (line_ref[base + 2 * cap] + burst - 1) // burst)
        def _(j):
            first = j * burst
            lines = wide_ref[pl.ds(pl.multiple_of(s * cap + first, burst), burst), :]
            for u in range(burst):
                bank = banks[u % len(banks)]
                at = pl.ds(line_ref[base + first + u], 1)
                bank[at, :] = bank[at, :] + lines[u : u + 1]

    def leave(j):
        to = pl.ds(pl.multiple_of(j * 8 * BLOCK, 8 * BLOCK), 8 * BLOCK)
        return pltpu.make_async_copy(out_ref.at[:, to], out_hbm.at[:, to], out_sem)

    @pl.loop(0, rows // BLOCK)
    def _(j):
        at = pl.ds(pl.multiple_of(j * BLOCK, BLOCK), BLOCK)
        total = banks[0][at, :]
        for bank in banks[1:]:
            total = total + bank[at, :]
        turned = jnp.transpose(total)
        for k in range(8):
            to = pl.ds(pl.multiple_of((j * 8 + k) * BLOCK, BLOCK), BLOCK)
            out_ref[:, to] = turned[k * 16 : k * 16 + CH]
        leave(j).start()

    pltpu.make_async_copy(out_ref, out_hbm, out_sem).wait()


def body(splat_params, list_owner, list_slot, list_length, target):
    devices = lax.axis_size(("row", "col"))
    tiles, slots = list_slot.shape
    entries = tiles * slots
    splats = splat_params.shape[1]
    pixels = target.shape[2]
    cap = 2 * entries // devices
    total = devices * cap
    rows = splats // 8
    smem = pl.BlockSpec(memory_space=pltpu.SMEM)
    vmem = pl.BlockSpec(memory_space=pltpu.VMEM)
    rendered, asked, incoming, coming = pl.pallas_call(
        step_kernel,
        in_specs=[smem, vmem, vmem, vmem, pl.BlockSpec(memory_space=pl.ANY)],
        out_specs=(vmem, vmem, vmem, vmem),
        out_shape=(
            jax.ShapeDtypeStruct((4, tiles, pixels), F32),
            jax.ShapeDtypeStruct((devices, 1, 2 * cap + 128), jnp.int32),
            jax.ShapeDtypeStruct((devices, 8, cap), F32),
            jax.ShapeDtypeStruct((devices, CH - 8, cap), F32),
        ),
        scratch_shapes=[
            pltpu.VMEM((CH, splats), F32),
            pltpu.VMEM((rows, 128), F32),
            pltpu.VMEM((128, BLOCK), F32),
            pltpu.VMEM((cap, 128), F32),
            pltpu.VMEM((cap, 128), F32),
            pltpu.SMEM((devices, 1, 2 * cap + 128), jnp.int32),
            pltpu.VMEM((tiles, 1, slots), jnp.int32),
            pltpu.VMEM((tiles, 1, slots), jnp.int32),
            pltpu.VMEM((devices, 1, 2 * cap + 128), jnp.int32),
            pltpu.VMEM((devices, 8, cap), F32),
            pltpu.VMEM((devices, CH - 8, cap), F32),
            pltpu.VMEM((devices, 8, cap), F32),
            pltpu.VMEM((devices, CH - 8, cap), F32),
            pltpu.VMEM((devices, 8, cap), F32),
            pltpu.VMEM((devices, CH - 8, cap), F32),
            pltpu.VMEM((CH * devices, 2 * cap), BF16),
            pltpu.VMEM((CH * devices, cap), F32),
            pltpu.VMEM((16, slots), F32),
            pltpu.VMEM((16, slots), F32),
            pltpu.VMEM((pixels, slots), F32),
            pltpu.VMEM((pixels, slots), F32),
            pltpu.VMEM((pixels, 2 * SB), BF16),
            pltpu.VMEM((pixels, SB), F32),
            pltpu.VMEM((pixels, SB), F32),
            pltpu.VMEM((CH * devices, 2 * slots), BF16),
            pltpu.VMEM((pixels, slots), BF16),
            pltpu.VMEM((pixels, slots), BF16),
            pltpu.SemaphoreType.DMA((2,)),
            pltpu.SemaphoreType.DMA((5,)),
            pltpu.SemaphoreType.DMA((5,)),
        ],
        compiler_params=pltpu.CompilerParams(collective_id=0, has_side_effects=True),
        name="step",
    )(list_length, list_owner.reshape(tiles, 1, slots), list_slot, target, splat_params)
    splat_grads = pl.pallas_call(
        scatter_kernel,
        in_specs=[smem, vmem, vmem, vmem],
        out_specs=pl.BlockSpec(memory_space=pl.ANY),
        out_shape=jax.ShapeDtypeStruct((CH, splats), F32),
        scratch_shapes=[
            pltpu.VMEM((total, 128), F32),
            pltpu.VMEM((CH, splats), F32),
            pltpu.SemaphoreType.DMA,
        ]
        + [pltpu.VMEM((rows, 128), F32)] * 4,
        name="accumulate",
    )(asked.reshape(-1), asked, incoming, coming)
    return (rendered, splat_grads)


def solution(mesh):
    in_specs = (
        P(None, ("row", "col")),
        P(("row", "col"), None, None),
        P(("row", "col"), None),
        P(("row", "col")),
        P(None, ("row", "col"), None),
    )
    out_specs = (P(None, ("row", "col"), None), P(None, ("row", "col")))
    return jax.shard_map(body, mesh=mesh, in_specs=in_specs, out_specs=out_specs, check_vma=False)
```

```python
import functools

import jax
import jax.numpy as jnp
from jax import lax
from jax.experimental import pallas as pl
from jax.experimental.pallas import tpu as pltpu
from jax.sharding import PartitionSpec as P

SIDE = 16
SB = 256
CH = 10
F32 = jnp.float32
BF16 = jnp.bfloat16
NT = (((1,), (1,)), ((), ()))
BLOCK = 512
LOG2E = 1.4426950408889634


def iota(shape, dim):
    return lax.broadcasted_iota(jnp.int32, shape, dim)


def split(x):
    high = x.astype(BF16)
    return high, (x - high.astype(F32)).astype(BF16)


def mm(a, b):
    return jnp.dot(a, b, preferred_element_type=F32)


def mm_nt(a, b):
    return lax.dot_general(a, b, NT, preferred_element_type=F32)


def one_hot(index, size):
    return jnp.where(iota((size, index.shape[1]), 0) == index, 1.0, 0.0).astype(BF16)


def step_kernel(
    length_ref, own_ref, slot_ref, target_ref, params_hbm, image_ref, asked_ref, incoming_ref, coming_ref,
    params_ref, table_ref, wide_ref, even_ref, odd_ref, lines_ref, live_ref, rank_ref, req_ref,
    found_ref, find_ref, replies_ref, reply_ref, outgoing_ref, going_ref, reply_both, sent_ref,
    vals, grads, falloff_ref, trans_ref, both_ref, shade_ref, after_ref, pack_ref, heavy_ref, light_ref,
    local_sem, send_sem, recv_sem,
):
    rows_on = lax.axis_size("row")
    cols_on = lax.axis_size("col")
    devices = rows_on * cols_on
    me = lax.axis_index("row") * cols_on + lax.axis_index("col")
    tiles, slots = slot_ref.shape
    cap = found_ref.shape[2]
    pixels = target_ref.shape[2]
    rows = table_ref.shape[0]
    others = pl.ds(0, devices - 1)

    half = devices // 2

    def peer(k):
        return lax.rem(me + half + k - 1 + (k - 1) // half, devices)

    def place_of(device):
        return (device // cols_on, lax.rem(device, cols_on))

    def push(device, source, target, phase):
        return pltpu.make_async_remote_copy(
            src_ref=source.at[device],
            dst_ref=target.at[me],
            send_sem=send_sem.at[phase],
            recv_sem=recv_sem.at[phase],
            device_id=place_of(device),
            device_id_type=pl.DeviceIdType.MESH,
        )

    def drain(source, target, phase):
        pltpu.make_async_copy(target.at[others], target.at[others], recv_sem.at[phase]).wait()
        pltpu.make_async_copy(source.at[others], source.at[others], send_sem.at[phase]).wait()

    barrier = pltpu.get_barrier_semaphore()

    @pl.loop(1, devices)
    def _(k):
        pl.semaphore_signal(
            barrier, inc=1, device_id=place_of(peer(k)), device_id_type=pl.DeviceIdType.MESH
        )

    load = pltpu.make_async_copy(params_hbm, params_ref, local_sem.at[0])
    load.start()

    strict = jnp.where(iota((SB, SB), 0) < iota((SB, SB), 1), 1.0, 0.0).astype(BF16)
    later = jnp.where(iota((SB, SB), 0) > iota((SB, SB), 1), 1.0, 0.0).astype(BF16)
    strict_twice = jnp.concatenate([strict, strict], axis=0)
    later_twice = jnp.concatenate([later, later], axis=0)
    count = jnp.zeros((devices, 1), F32)
    high = jnp.zeros((devices, cap), F32)
    low = jnp.zeros((devices, cap), F32)
    for tile in range(tiles):
        for j in range(slots // SB):
            part = slice(j * SB, (j + 1) * SB)
            owner = jnp.where(iota((1, SB), 1) + j * SB < length_ref[tile], own_ref[tile, :, part], -1)
            live_ref[tile, :, part] = owner
            mine = iota((devices, SB), 0) == owner
            ones = jnp.where(mine, 1.0, 0.0)
            ahead = mm(ones.astype(BF16), strict) + count
            rank = jnp.sum(ones * ahead, axis=0, keepdims=True).astype(jnp.int32)
            count = count + jnp.sum(ones, axis=1, keepdims=True)
            rank_ref[tile, :, part] = rank
            named = slot_ref[tile : tile + 1, part]
            places = one_hot(rank, cap)
            slot_high = (named >> 8).astype(F32)
            slot_low = ((named & 255) + 1).astype(F32)
            high = high + mm_nt(jnp.where(mine, slot_high, 0.0).astype(BF16), places)
            low = low + mm_nt(jnp.where(mine, slot_low, 0.0).astype(BF16), places)
    wanted = (high * 256.0 + low).astype(jnp.int32) - 1
    chunk = wanted >> (8 * BLOCK).bit_length() - 1
    line = (chunk & (rows // BLOCK - 1)) * BLOCK + (wanted & (BLOCK - 1))
    group = jnp.where(wanted < 0, -1, (wanted >> BLOCK.bit_length() - 1) & 7)
    filled = jnp.broadcast_to(count, (devices, 128)).astype(jnp.int32)
    for d in range(devices):
        req_ref[d, :, :cap] = line[d : d + 1]
        req_ref[d, :, cap : 2 * cap] = group[d : d + 1]
        req_ref[d, :, 2 * cap :] = filled[d : d + 1]
    pl.semaphore_wait(barrier, devices - 1)

    @pl.loop(1, devices)
    def _(k):
        push(peer(k), req_ref, asked_ref, 0).start()

    asked_ref[me] = req_ref[me]
    load.wait()
    wide_ref[...] = jnp.zeros_like(wide_ref)

    @pl.loop(0, rows // BLOCK)
    def _(j):
        for k in range(8):
            at = pl.ds(pl.multiple_of((j * 8 + k) * BLOCK, BLOCK), BLOCK)
            wide_ref[k * 16 : k * 16 + CH, :] = params_ref[:, at]
        table_ref[pl.ds(pl.multiple_of(j * BLOCK, BLOCK), BLOCK), :] = jnp.transpose(wide_ref[...])

    drain(req_ref, asked_ref, 0)
    move = pltpu.make_async_copy(asked_ref, lines_ref, local_sem.at[1])
    move.start()
    move.wait()

    eye = jnp.where(iota((128, 128), 0) == iota((128, 128), 1), 1.0, 0.0).astype(BF16)

    def fetch(source, held):
        for j in range(cap):
            held[j : j + 1, :] = table_ref[pl.ds(lines_ref[source, 0, j], 1), :]

    def pick(source, held):
        high, low = split(held[...])
        turned = mm_nt(eye, high) + mm_nt(eye, low)
        group = asked_ref[source, :, cap : 2 * cap]
        found = jnp.zeros((16, cap), F32)
        for q in range(8):
            found = found + jnp.where(group == q, turned[q * 16 : q * 16 + 16], 0.0)
        return found[:8], found[8:CH]

    def answer(source, held):
        found_ref[source], find_ref[source] = pick(source, held)
        push(source, found_ref, replies_ref, 1).start()
        push(source, find_ref, reply_ref, 2).start()

    fetch(peer(1), even_ref)

    @pl.loop(0, devices // 2 - 1)
    def _(p):
        fetch(peer(2 * p + 2), odd_ref)
        answer(peer(2 * p + 1), even_ref)
        fetch(peer(2 * p + 3), even_ref)
        answer(peer(2 * p + 2), odd_ref)

    answer(peer(devices - 1), even_ref)
    fetch(me, odd_ref)
    replies_ref[me], reply_ref[me] = pick(me, odd_ref)
    drain(found_ref, replies_ref, 1)
    drain(find_ref, reply_ref, 2)

    for ch in range(CH):
        part = slice(ch * devices, (ch + 1) * devices)
        reply_both[part, :cap], reply_both[part, cap:] = split(replies_ref[:, ch, :] if ch < 8 else reply_ref[:, ch - 8, :])
    sent_ref[...] = jnp.zeros_like(sent_ref)
    blocks = slots // SB
    centres = iota((SIDE, SB), 0).astype(F32) + 0.5
    side_rows = pixels // SIDE

    @pl.loop(0, tiles)
    def _(tile):
        length = length_ref[tile]
        mine = iota((devices, slots), 0) == live_ref[tile]
        places = one_hot(rank_ref[tile], cap)
        fetched = mm(reply_both[...], jnp.concatenate([places, places], axis=0))
        vals[...] = jnp.zeros_like(vals)
        live = jnp.where(iota((1, slots), 1) < length, 1.0, 0.0)
        for ch in range(CH):
            part = slice(ch * devices, (ch + 1) * devices)
            value = jnp.sum(jnp.where(mine, fetched[part], 0.0), axis=0, keepdims=True)
            if ch == 5:
                value = value * live
            row = ch if ch < 6 else ch + 2
            vals[row : row + 1, :] = value

        carry = jnp.zeros((pixels, 1), F32)
        image = jnp.zeros((pixels, 16), F32)
        image_light = jnp.zeros((pixels, 8), F32)
        for blk in range(blocks):
            at = slice(blk * SB, (blk + 1) * SB)
            dx = centres - vals[0:1, at]
            dy = centres - vals[1:2, at]
            ex = (-0.5 * LOG2E) * vals[2:3, at] * dx * dx
            ey = (-0.5 * LOG2E) * vals[4:5, at] * dy * dy
            bdy = -LOG2E * vals[3:4, at] * dy
            opacity = vals[5:6, at]
            for y in range(side_rows):
                rows_at = slice(y * SIDE, (y + 1) * SIDE)
                falloff = jnp.exp2(ex + ey[y : y + 1] + dx * bdy[y : y + 1])
                falloff_ref[rows_at, at] = falloff
                both_ref[rows_at, :SB], both_ref[rows_at, SB:] = split(jnp.log2(1.0 - opacity * falloff))
            total = mm(both_ref[...], strict_twice) + carry
            last = both_ref[:, SB - 128 : SB].astype(F32) + both_ref[:, 2 * SB - 128 :].astype(F32)
            carry = total[:, SB - 1 : SB] + last[:, 127:128]
            trans = jnp.exp2(total)
            trans_ref[:, at] = trans
            weight_high, weight_low = split(trans * (opacity * falloff_ref[:, at]))
            heavy_ref[:, at] = weight_high
            light_ref[:, at] = weight_low
            colour_high, colour_low = split(vals[8:16, at])
            image = image + mm_nt(weight_high, jnp.concatenate([colour_high, colour_low], axis=0))
            image_light = image_light + mm_nt(weight_low, colour_high)
        turned_image = jnp.transpose(image)
        rendered = turned_image[:8] + turned_image[8:] + jnp.transpose(image_light)
        for ch in range(4):
            image_ref[ch, pl.ds(tile, 1), :] = rendered[ch : ch + 1]
        wished = [target_ref[ch, pl.ds(tile, 1), :] for ch in range(4)]
        wished = jnp.concatenate(wished + [jnp.zeros((4, pixels), F32)], axis=0)
        grad_image = 2.0 * (rendered - wished)
        grad_high, grad_low = split(grad_image)
        grad_wide = grad_high.astype(F32)
        grad_rest = grad_image - grad_wide
        turned = jnp.transpose(jnp.concatenate([grad_wide, grad_wide, grad_rest, grad_image], axis=0))
        turned_parts = turned.astype(BF16)
        grad_both = jnp.concatenate([grad_high, grad_low], axis=0)

        spent = jnp.zeros((pixels, 1), F32)
        for blk in reversed(range(blocks)):
            at = slice(blk * SB, (blk + 1) * SB)
            mean_x, mean_y = vals[0:1, at], vals[1:2, at]
            conic_a, conic_b, conic_c = vals[2:3, at], vals[3:4, at], vals[4:5, at]
            opacity = vals[5:6, at]
            dx = centres - mean_x
            dy = centres - mean_y
            colours = vals[8:16, at]
            colour_wide = colours.astype(BF16).astype(F32)
            colour_parts = jnp.concatenate(
                [colour_wide, colours - colour_wide, colour_wide, jnp.zeros_like(colours)], axis=0
            ).astype(BF16)
            shading = mm(turned_parts, colour_parts)
            shade_ref[...] = shading
            colour_grads = mm(grad_both, heavy_ref[:, at])
            grads[8:16, at] = colour_grads[:8] + colour_grads[8:] + mm(grad_high, light_ref[:, at])
            gain = trans_ref[:, at] * (opacity * falloff_ref[:, at]) * shading
            both_ref[:, :SB], both_ref[:, SB:] = split(gain)
            after = mm(both_ref[...], later_twice) + spent
            spent = after[:, 0:1] + gain[:, 0:1]
            after_ref[...] = after
            moment0 = jnp.zeros((SIDE, SB), F32)
            moment1 = moment0
            moment2 = moment0
            for y in range(side_rows):
                rows_at = slice(y * SIDE, (y + 1) * SIDE)
                falloff = falloff_ref[rows_at, at]
                grad_alpha = trans_ref[rows_at, at] * shade_ref[rows_at, :] - after_ref[rows_at, :] / (
                    1.0 - opacity * falloff
                )
                opaque = grad_alpha * falloff
                moment0 = moment0 + opaque
                lever = opaque * dy[y : y + 1]
                moment1 = moment1 + lever
                moment2 = moment2 + lever * dy[y : y + 1]
            across = moment0 * dx
            sum_x = jnp.sum(across, axis=0, keepdims=True)
            sum_y = jnp.sum(moment1, axis=0, keepdims=True)
            grads[0:1, at] = opacity * (conic_a * sum_x + conic_b * sum_y)
            grads[1:2, at] = opacity * (conic_c * sum_y + conic_b * sum_x)
            grads[2:3, at] = -0.5 * opacity * jnp.sum(across * dx, axis=0, keepdims=True)
            grads[3:4, at] = -opacity * jnp.sum(moment1 * dx, axis=0, keepdims=True)
            grads[4:5, at] = -0.5 * opacity * jnp.sum(moment2, axis=0, keepdims=True)
            grads[5:6, at] = jnp.sum(moment0, axis=0, keepdims=True) * live[:, at]

        for ch in range(CH):
            part = slice(ch * devices, (ch + 1) * devices)
            row = ch if ch < 6 else ch + 2
            high, low = split(jnp.where(mine, grads[row : row + 1, :], 0.0))
            pack_ref[part, :slots] = high
            pack_ref[part, slots:] = low
        sent = mm_nt(pack_ref[...], jnp.concatenate([places, places], axis=1))

        sent_ref[...] += sent

    for ch in range(CH):
        part = slice(ch * devices, (ch + 1) * devices)
        if ch < 8:
            outgoing_ref[:, ch, :] = sent_ref[part, :]
        else:
            going_ref[:, ch - 8, :] = sent_ref[part, :]

    @pl.loop(1, devices)
    def _(k):
        push(peer(k), outgoing_ref, incoming_ref, 3).start()
        push(peer(k), going_ref, coming_ref, 4).start()

    incoming_ref[me] = outgoing_ref[me]
    coming_ref[me] = going_ref[me]
    drain(outgoing_ref, incoming_ref, 3)
    drain(going_ref, coming_ref, 4)


def scatter_kernel(
    line_ref, ask_ref, grad_ref, rest_ref, out_hbm, wide_ref, out_ref, out_sem, *banks
):
    rows = banks[0].shape[0]
    devices, _, cap = grad_ref.shape
    share = rows // devices
    burst = 32

    @pl.loop(0, devices // 2)
    def _(p):
        wides = []
        for s in (2 * p, 2 * p + 1):
            group = ask_ref[s, :, cap : 2 * cap]
            parts = [grad_ref[s], rest_ref[s], jnp.zeros((16 - CH, cap), F32)]
            grad = jnp.concatenate(parts, axis=0)
            wides.append(jnp.concatenate([jnp.where(group == k, grad, 0.0) for k in range(8)], axis=0))
        lines = [jnp.transpose(wide) for wide in wides]
        at = pl.ds(pl.multiple_of(p * 2 * share, 2 * share), 2 * share)
        for bank in banks:
            bank[at, :] = jnp.zeros((2 * share, 128), F32)
        for k, line in enumerate(lines):
            wide_ref[pl.ds(pl.multiple_of((2 * p + k) * cap, cap), cap), :] = line

    @pl.loop(0, devices)
    def _(s):
        base = s * (line_ref.shape[0] // devices)

        @pl.loop(0, (line_ref[base + 2 * cap] + burst - 1) // burst)
        def _(j):
            first = j * burst
            lines = wide_ref.at[pl.ds(pl.multiple_of(s * cap + first, burst), burst), :]
            for u in range(burst):
                bank = banks[u % len(banks)]
                at = pl.ds(line_ref[base + first + u], 1)
                bank[at, :] = bank[at, :] + lines[u : u + 1, :]

    def leave(j):
        to = pl.ds(pl.multiple_of(j * 8 * BLOCK, 8 * BLOCK), 8 * BLOCK)
        return pltpu.make_async_copy(out_ref.at[:, to], out_hbm.at[:, to], out_sem)

    @pl.loop(0, rows // BLOCK, unroll=2)
    def _(j):
        at = pl.ds(pl.multiple_of(j * BLOCK, BLOCK), BLOCK)
        total = banks[0][at, :]
        for bank in banks[1:]:
            total = total + bank[at, :]
        turned = jnp.transpose(total)
        for k in range(8):
            to = pl.ds(pl.multiple_of((j * 8 + k) * BLOCK, BLOCK), BLOCK)
            out_ref[:, to] = turned[k * 16 : k * 16 + CH]
        leave(j).start()

    pltpu.make_async_copy(out_ref, out_hbm, out_sem).wait()


def body(splat_params, list_owner, list_slot, list_length, target):
    devices = lax.axis_size(("row", "col"))
    tiles, slots = list_slot.shape
    entries = tiles * slots
    splats = splat_params.shape[1]
    pixels = target.shape[2]
    cap = 2 * entries // devices
    total = devices * cap
    rows = splats // 8
    smem = pl.BlockSpec(memory_space=pltpu.SMEM)
    vmem = pl.BlockSpec(memory_space=pltpu.VMEM)
    rendered, asked, incoming, coming = pl.pallas_call(
        step_kernel,
        in_specs=[smem, vmem, vmem, vmem, pl.BlockSpec(memory_space=pl.ANY)],
        out_specs=(vmem, vmem, vmem, vmem),
        out_shape=(
            jax.ShapeDtypeStruct((4, tiles, pixels), F32),
            jax.ShapeDtypeStruct((devices, 1, 2 * cap + 128), jnp.int32),
            jax.ShapeDtypeStruct((devices, 8, cap), F32),
            jax.ShapeDtypeStruct((devices, CH - 8, cap), F32),
        ),
        scratch_shapes=[
            pltpu.VMEM((CH, splats), F32),
            pltpu.VMEM((rows, 128), F32),
            pltpu.VMEM((128, BLOCK), F32),
            pltpu.VMEM((cap, 128), F32),
            pltpu.VMEM((cap, 128), F32),
            pltpu.SMEM((devices, 1, 2 * cap + 128), jnp.int32),
            pltpu.VMEM((tiles, 1, slots), jnp.int32),
            pltpu.VMEM((tiles, 1, slots), jnp.int32),
            pltpu.VMEM((devices, 1, 2 * cap + 128), jnp.int32),
            pltpu.VMEM((devices, 8, cap), F32),
            pltpu.VMEM((devices, CH - 8, cap), F32),
            pltpu.VMEM((devices, 8, cap), F32),
            pltpu.VMEM((devices, CH - 8, cap), F32),
            pltpu.VMEM((devices, 8, cap), F32),
            pltpu.VMEM((devices, CH - 8, cap), F32),
            pltpu.VMEM((CH * devices, 2 * cap), BF16),
            pltpu.VMEM((CH * devices, cap), F32),
            pltpu.VMEM((16, slots), F32),
            pltpu.VMEM((16, slots), F32),
            pltpu.VMEM((pixels, slots), F32),
            pltpu.VMEM((pixels, slots), F32),
            pltpu.VMEM((pixels, 2 * SB), BF16),
            pltpu.VMEM((pixels, SB), F32),
            pltpu.VMEM((pixels, SB), F32),
            pltpu.VMEM((CH * devices, 2 * slots), BF16),
            pltpu.VMEM((pixels, slots), BF16),
            pltpu.VMEM((pixels, slots), BF16),
            pltpu.SemaphoreType.DMA((2,)),
            pltpu.SemaphoreType.DMA((5,)),
            pltpu.SemaphoreType.DMA((5,)),
        ],
        compiler_params=pltpu.CompilerParams(collective_id=0, has_side_effects=True),
        name="step",
    )(list_length, list_owner.reshape(tiles, 1, slots), list_slot, target, splat_params)
    splat_grads = pl.pallas_call(
        scatter_kernel,
        in_specs=[smem, vmem, vmem, vmem],
        out_specs=pl.BlockSpec(memory_space=pl.ANY),
        out_shape=jax.ShapeDtypeStruct((CH, splats), F32),
        scratch_shapes=[
            pltpu.VMEM((total, 128), F32),
            pltpu.VMEM((CH, splats), F32),
            pltpu.SemaphoreType.DMA,
        ]
        + [pltpu.VMEM((rows, 128), F32)] * 4,
        name="accumulate",
    )(asked.reshape(-1), asked, incoming, coming)
    return (rendered, splat_grads)


def solution(mesh):
    in_specs = (
        P(None, ("row", "col")),
        P(("row", "col"), None, None),
        P(("row", "col"), None),
        P(("row", "col")),
        P(None, ("row", "col"), None),
    )
    out_specs = (P(None, ("row", "col"), None), P(None, ("row", "col")))
    return jax.shard_map(body, mesh=mesh, in_specs=in_specs, out_specs=out_specs, check_vma=False)
```

```python
import functools

import jax
import jax.numpy as jnp
from jax import lax
from jax.experimental import pallas as pl
from jax.experimental.pallas import tpu as pltpu
from jax.sharding import PartitionSpec as P

SIDE = 16
SB = 256
CH = 10
F32 = jnp.float32
BF16 = jnp.bfloat16
NT = (((1,), (1,)), ((), ()))
BLOCK = 512
LOG2E = 1.4426950408889634


def iota(shape, dim):
    return lax.broadcasted_iota(jnp.int32, shape, dim)


def split(x):
    high = x.astype(BF16)
    return high, (x - high.astype(F32)).astype(BF16)


def mm(a, b):
    return jnp.dot(a, b, preferred_element_type=F32)


def mm_nt(a, b):
    return lax.dot_general(a, b, NT, preferred_element_type=F32)


def one_hot(index, size):
    return jnp.where(iota((size, index.shape[1]), 0) == index, 1.0, 0.0).astype(BF16)


def step_kernel(
    length_ref, own_ref, slot_ref, target_ref, params_hbm, image_ref, asked_ref, incoming_ref, coming_ref,
    params_ref, table_ref, wide_ref, even_ref, odd_ref, lines_ref, live_ref, rank_ref, req_ref,
    found_ref, find_ref, replies_ref, reply_ref, outgoing_ref, going_ref, reply_both, sent_ref,
    vals, grads, falloff_ref, trans_ref, both_ref, shade_ref, after_ref, pack_ref, heavy_ref, light_ref,
    local_sem, send_sem, recv_sem,
):
    rows_on = lax.axis_size("row")
    cols_on = lax.axis_size("col")
    devices = rows_on * cols_on
    me = lax.axis_index("row") * cols_on + lax.axis_index("col")
    tiles, slots = slot_ref.shape
    cap = found_ref.shape[2]
    pixels = target_ref.shape[2]
    rows = table_ref.shape[0]
    others = pl.ds(0, devices - 1)

    def peer(k):
        return lax.rem(me + k, devices)

    def place_of(device):
        return (device // cols_on, lax.rem(device, cols_on))

    def push(device, source, target, phase):
        return pltpu.make_async_remote_copy(
            src_ref=source.at[device],
            dst_ref=target.at[me],
            send_sem=send_sem.at[phase],
            recv_sem=recv_sem.at[phase],
            device_id=place_of(device),
            device_id_type=pl.DeviceIdType.MESH,
        )

    def drain(source, target, phase):
        pltpu.make_async_copy(target.at[others], target.at[others], recv_sem.at[phase]).wait()
        pltpu.make_async_copy(source.at[others], source.at[others], send_sem.at[phase]).wait()

    barrier = pltpu.get_barrier_semaphore()

    @pl.loop(1, devices)
    def _(k):
        pl.semaphore_signal(
            barrier, inc=1, device_id=place_of(peer(k)), device_id_type=pl.DeviceIdType.MESH
        )

    load = pltpu.make_async_copy(params_hbm, params_ref, local_sem.at[0])
    load.start()

    strict = jnp.where(iota((SB, SB), 0) < iota((SB, SB), 1), 1.0, 0.0).astype(BF16)
    later = jnp.where(iota((SB, SB), 0) > iota((SB, SB), 1), 1.0, 0.0).astype(BF16)
    strict_twice = jnp.concatenate([strict, strict], axis=0)
    later_twice = jnp.concatenate([later, later], axis=0)
    count = jnp.zeros((devices, 1), F32)
    high = jnp.zeros((devices, cap), F32)
    low = jnp.zeros((devices, cap), F32)
    for tile in range(tiles):
        for j in range(slots // SB):
            part = slice(j * SB, (j + 1) * SB)
            owner = jnp.where(iota((1, SB), 1) + j * SB < length_ref[tile], own_ref[tile, :, part], -1)
            live_ref[tile, :, part] = owner
            mine = iota((devices, SB), 0) == owner
            ones = jnp.where(mine, 1.0, 0.0)
            ahead = mm(ones.astype(BF16), strict) + count
            rank = jnp.sum(ones * ahead, axis=0, keepdims=True).astype(jnp.int32)
            count = count + jnp.sum(ones, axis=1, keepdims=True)
            rank_ref[tile, :, part] = rank
            named = slot_ref[tile : tile + 1, part]
            places = one_hot(rank, cap)
            slot_high = (named >> 8).astype(F32)
            slot_low = ((named & 255) + 1).astype(F32)
            high = high + mm_nt(jnp.where(mine, slot_high, 0.0).astype(BF16), places)
            low = low + mm_nt(jnp.where(mine, slot_low, 0.0).astype(BF16), places)
    wanted = (high * 256.0 + low).astype(jnp.int32) - 1
    chunk = wanted >> (8 * BLOCK).bit_length() - 1
    line = (chunk & (rows // BLOCK - 1)) * BLOCK + (wanted & (BLOCK - 1))
    group = jnp.where(wanted < 0, -1, (wanted >> BLOCK.bit_length() - 1) & 7)
    filled = jnp.broadcast_to(count, (devices, 128)).astype(jnp.int32)
    for d in range(devices):
        req_ref[d, :, :cap] = line[d : d + 1]
        req_ref[d, :, cap : 2 * cap] = group[d : d + 1]
        req_ref[d, :, 2 * cap :] = filled[d : d + 1]
    pl.semaphore_wait(barrier, devices - 1)

    @pl.loop(1, devices)
    def _(k):
        push(peer(k), req_ref, asked_ref, 0).start()

    asked_ref[me] = req_ref[me]
    load.wait()
    wide_ref[...] = jnp.zeros_like(wide_ref)

    @pl.loop(0, rows // BLOCK)
    def _(j):
        for k in range(8):
            at = pl.ds(pl.multiple_of((j * 8 + k) * BLOCK, BLOCK), BLOCK)
            wide_ref[k * 16 : k * 16 + CH, :] = params_ref[:, at]
        table_ref[pl.ds(pl.multiple_of(j * BLOCK, BLOCK), BLOCK), :] = jnp.transpose(wide_ref[...])

    drain(req_ref, asked_ref, 0)
    move = pltpu.make_async_copy(asked_ref, lines_ref, local_sem.at[1])
    move.start()
    move.wait()

    eye = jnp.where(iota((128, 128), 0) == iota((128, 128), 1), 1.0, 0.0).astype(BF16)

    def fetch(source, held):
        for j in range(cap):
            held[j : j + 1, :] = table_ref[pl.ds(lines_ref[source, 0, j], 1), :]

    def pick(source, held):
        high, low = split(held[...])
        turned = mm_nt(eye, high) + mm_nt(eye, low)
        group = asked_ref[source, :, cap : 2 * cap]
        found = jnp.zeros((16, cap), F32)
        for q in range(8):
            found = found + jnp.where(group == q, turned[q * 16 : q * 16 + 16], 0.0)
        return found[:8], found[8:CH]

    def answer(source, held):
        found_ref[source], find_ref[source] = pick(source, held)
        push(source, found_ref, replies_ref, 1).start()
        push(source, find_ref, reply_ref, 2).start()

    fetch(peer(1), even_ref)

    @pl.loop(0, devices // 2 - 1)
    def _(p):
        fetch(peer(2 * p + 2), odd_ref)
        answer(peer(2 * p + 1), even_ref)
        fetch(peer(2 * p + 3), even_ref)
        answer(peer(2 * p + 2), odd_ref)

    answer(peer(devices - 1), even_ref)
    fetch(me, odd_ref)
    replies_ref[me], reply_ref[me] = pick(me, odd_ref)
    drain(found_ref, replies_ref, 1)
    drain(find_ref, reply_ref, 2)

    for ch in range(CH):
        part = slice(ch * devices, (ch + 1) * devices)
        reply_both[part, :cap], reply_both[part, cap:] = split(replies_ref[:, ch, :] if ch < 8 else reply_ref[:, ch - 8, :])
    sent_ref[...] = jnp.zeros_like(sent_ref)
    blocks = slots // SB
    centres = iota((SIDE, SB), 0).astype(F32) + 0.5
    side_rows = pixels // SIDE

    @pl.loop(0, tiles)
    def _(tile):
        length = length_ref[tile]
        mine = iota((devices, slots), 0) == live_ref[tile]
        places = one_hot(rank_ref[tile], cap)
        fetched = mm(reply_both[...], jnp.concatenate([places, places], axis=0))
        vals[...] = jnp.zeros_like(vals)
        live = jnp.where(iota((1, slots), 1) < length, 1.0, 0.0)
        for ch in range(CH):
            part = slice(ch * devices, (ch + 1) * devices)
            value = jnp.sum(jnp.where(mine, fetched[part], 0.0), axis=0, keepdims=True)
            if ch == 5:
                value = value * live
            row = ch if ch < 6 else ch + 2
            vals[row : row + 1, :] = value

        carry = jnp.zeros((pixels, 1), F32)
        image = jnp.zeros((pixels, 16), F32)
        image_light = jnp.zeros((pixels, 8), F32)
        for blk in range(blocks):
            at = slice(blk * SB, (blk + 1) * SB)
            dx = centres - vals[0:1, at]
            dy = centres - vals[1:2, at]
            ex = (-0.5 * LOG2E) * vals[2:3, at] * dx * dx
            ey = (-0.5 * LOG2E) * vals[4:5, at] * dy * dy
            bdy = -LOG2E * vals[3:4, at] * dy
            opacity = vals[5:6, at]
            for y in range(side_rows):
                rows_at = slice(y * SIDE, (y + 1) * SIDE)
                falloff = jnp.exp2(ex + ey[y : y + 1] + dx * bdy[y : y + 1])
                falloff_ref[rows_at, at] = falloff
                both_ref[rows_at, :SB], both_ref[rows_at, SB:] = split(jnp.log2(1.0 - opacity * falloff))
            total = mm(both_ref[...], strict_twice) + carry
            last = both_ref[:, SB - 128 : SB].astype(F32) + both_ref[:, 2 * SB - 128 :].astype(F32)
            carry = total[:, SB - 1 : SB] + last[:, 127:128]
            trans = jnp.exp2(total)
            trans_ref[:, at] = trans
            weight_high, weight_low = split(trans * (opacity * falloff_ref[:, at]))
            heavy_ref[:, at] = weight_high
            light_ref[:, at] = weight_low
            colour_high, colour_low = split(vals[8:16, at])
            image = image + mm_nt(weight_high, jnp.concatenate([colour_high, colour_low], axis=0))
            image_light = image_light + mm_nt(weight_low, colour_high)
        turned_image = jnp.transpose(image)
        rendered = turned_image[:8] + turned_image[8:] + jnp.transpose(image_light)
        for ch in range(4):
            image_ref[ch, pl.ds(tile, 1), :] = rendered[ch : ch + 1]
        wished = [target_ref[ch, pl.ds(tile, 1), :] for ch in range(4)]
        wished = jnp.concatenate(wished + [jnp.zeros((4, pixels), F32)], axis=0)
        grad_image = 2.0 * (rendered - wished)
        grad_high, grad_low = split(grad_image)
        grad_wide = grad_high.astype(F32)
        grad_rest = grad_image - grad_wide
        turned = jnp.transpose(jnp.concatenate([grad_wide, grad_wide, grad_rest, grad_image], axis=0))
        turned_parts = turned.astype(BF16)
        grad_both = jnp.concatenate([grad_high, grad_low], axis=0)

        spent = jnp.zeros((pixels, 1), F32)
        for blk in reversed(range(blocks)):
            at = slice(blk * SB, (blk + 1) * SB)
            mean_x, mean_y = vals[0:1, at], vals[1:2, at]
            conic_a, conic_b, conic_c = vals[2:3, at], vals[3:4, at], vals[4:5, at]
            opacity = vals[5:6, at]
            dx = centres - mean_x
            dy = centres - mean_y
            colours = vals[8:16, at]
            colour_wide = colours.astype(BF16).astype(F32)
            colour_parts = jnp.concatenate(
                [colour_wide, colours - colour_wide, colour_wide, jnp.zeros_like(colours)], axis=0
            ).astype(BF16)
            shading = mm(turned_parts, colour_parts)
            shade_ref[...] = shading
            colour_grads = mm(grad_both, heavy_ref[:, at])
            grads[8:16, at] = colour_grads[:8] + colour_grads[8:] + mm(grad_high, light_ref[:, at])
            gain = trans_ref[:, at] * (opacity * falloff_ref[:, at]) * shading
            both_ref[:, :SB], both_ref[:, SB:] = split(gain)
            after = mm(both_ref[...], later_twice) + spent
            spent = after[:, 0:1] + gain[:, 0:1]
            after_ref[...] = after
            moment0 = jnp.zeros((SIDE, SB), F32)
            moment1 = moment0
            moment2 = moment0
            for y in range(side_rows):
                rows_at = slice(y * SIDE, (y + 1) * SIDE)
                falloff = falloff_ref[rows_at, at]
                grad_alpha = trans_ref[rows_at, at] * shade_ref[rows_at, :] - after_ref[rows_at, :] / (
                    1.0 - opacity * falloff
                )
                opaque = grad_alpha * falloff
                moment0 = moment0 + opaque
                lever = opaque * dy[y : y + 1]
                moment1 = moment1 + lever
                moment2 = moment2 + lever * dy[y : y + 1]
            across = moment0 * dx
            sum_x = jnp.sum(across, axis=0, keepdims=True)
            sum_y = jnp.sum(moment1, axis=0, keepdims=True)
            grads[0:1, at] = opacity * (conic_a * sum_x + conic_b * sum_y)
            grads[1:2, at] = opacity * (conic_c * sum_y + conic_b * sum_x)
            grads[2:3, at] = -0.5 * opacity * jnp.sum(across * dx, axis=0, keepdims=True)
            grads[3:4, at] = -opacity * jnp.sum(moment1 * dx, axis=0, keepdims=True)
            grads[4:5, at] = -0.5 * opacity * jnp.sum(moment2, axis=0, keepdims=True)
            grads[5:6, at] = jnp.sum(moment0, axis=0, keepdims=True) * live[:, at]

        for ch in range(CH):
            part = slice(ch * devices, (ch + 1) * devices)
            row = ch if ch < 6 else ch + 2
            high, low = split(jnp.where(mine, grads[row : row + 1, :], 0.0))
            pack_ref[part, :slots] = high
            pack_ref[part, slots:] = low
        sent = mm_nt(pack_ref[...], jnp.concatenate([places, places], axis=1))

        sent_ref[...] += sent

    for ch in range(CH):
        part = slice(ch * devices, (ch + 1) * devices)
        if ch < 8:
            outgoing_ref[:, ch, :] = sent_ref[part, :]
        else:
            going_ref[:, ch - 8, :] = sent_ref[part, :]

    @pl.loop(1, devices)
    def _(k):
        push(peer(k), outgoing_ref, incoming_ref, 3).start()
        push(peer(k), going_ref, coming_ref, 4).start()

    incoming_ref[me] = outgoing_ref[me]
    coming_ref[me] = going_ref[me]
    drain(outgoing_ref, incoming_ref, 3)
    drain(going_ref, coming_ref, 4)


def scatter_kernel(
    line_ref, ask_ref, grad_ref, rest_ref, out_hbm, wide_ref, out_ref, out_sem, *banks
):
    rows = banks[0].shape[0]
    devices, _, cap = grad_ref.shape
    share = rows // devices
    burst = 32

    @pl.loop(0, devices // 2)
    def _(p):
        wides = []
        for s in (2 * p, 2 * p + 1):
            group = ask_ref[s, :, cap : 2 * cap]
            parts = [grad_ref[s], rest_ref[s], jnp.zeros((16 - CH, cap), F32)]
            grad = jnp.concatenate(parts, axis=0)
            wides.append(jnp.concatenate([jnp.where(group == k, grad, 0.0) for k in range(8)], axis=0))
        lines = [jnp.transpose(wide) for wide in wides]
        at = pl.ds(pl.multiple_of(p * 2 * share, 2 * share), 2 * share)
        for bank in banks:
            bank[at, :] = jnp.zeros((2 * share, 128), F32)
        for k, line in enumerate(lines):
            wide_ref[pl.ds(pl.multiple_of((2 * p + k) * cap, cap), cap), :] = line

    @pl.loop(0, devices)
    def _(s):
        base = s * (line_ref.shape[0] // devices)

        @pl.loop(0, (line_ref[base + 2 * cap] + burst - 1) // burst)
        def _(j):
            first = j * burst
            lines = wide_ref.at[pl.ds(pl.multiple_of(s * cap + first, burst), burst), :]
            for u in range(burst):
                bank = banks[u % len(banks)]
                at = pl.ds(line_ref[base + first + u], 1)
                bank[at, :] = bank[at, :] + lines[u : u + 1, :]

    def leave(j):
        to = pl.ds(pl.multiple_of(j * 8 * BLOCK, 8 * BLOCK), 8 * BLOCK)
        return pltpu.make_async_copy(out_ref.at[:, to], out_hbm.at[:, to], out_sem)

    @pl.loop(0, rows // BLOCK, unroll=2)
    def _(j):
        at = pl.ds(pl.multiple_of(j * BLOCK, BLOCK), BLOCK)
        total = banks[0][at, :]
        for bank in banks[1:]:
            total = total + bank[at, :]
        turned = jnp.transpose(total)
        for k in range(8):
            to = pl.ds(pl.multiple_of((j * 8 + k) * BLOCK, BLOCK), BLOCK)
            out_ref[:, to] = turned[k * 16 : k * 16 + CH]
        leave(j).start()

    pltpu.make_async_copy(out_ref, out_hbm, out_sem).wait()


def body(splat_params, list_owner, list_slot, list_length, target):
    devices = lax.axis_size(("row", "col"))
    tiles, slots = list_slot.shape
    entries = tiles * slots
    splats = splat_params.shape[1]
    pixels = target.shape[2]
    cap = 2 * entries // devices
    total = devices * cap
    rows = splats // 8
    smem = pl.BlockSpec(memory_space=pltpu.SMEM)
    vmem = pl.BlockSpec(memory_space=pltpu.VMEM)
    rendered, asked, incoming, coming = pl.pallas_call(
        step_kernel,
        in_specs=[smem, vmem, vmem, vmem, pl.BlockSpec(memory_space=pl.ANY)],
        out_specs=(vmem, vmem, vmem, vmem),
        out_shape=(
            jax.ShapeDtypeStruct((4, tiles, pixels), F32),
            jax.ShapeDtypeStruct((devices, 1, 2 * cap + 128), jnp.int32),
            jax.ShapeDtypeStruct((devices, 8, cap), F32),
            jax.ShapeDtypeStruct((devices, CH - 8, cap), F32),
        ),
        scratch_shapes=[
            pltpu.VMEM((CH, splats), F32),
            pltpu.VMEM((rows, 128), F32),
            pltpu.VMEM((128, BLOCK), F32),
            pltpu.VMEM((cap, 128), F32),
            pltpu.VMEM((cap, 128), F32),
            pltpu.SMEM((devices, 1, 2 * cap + 128), jnp.int32),
            pltpu.VMEM((tiles, 1, slots), jnp.int32),
            pltpu.VMEM((tiles, 1, slots), jnp.int32),
            pltpu.VMEM((devices, 1, 2 * cap + 128), jnp.int32),
            pltpu.VMEM((devices, 8, cap), F32),
            pltpu.VMEM((devices, CH - 8, cap), F32),
            pltpu.VMEM((devices, 8, cap), F32),
            pltpu.VMEM((devices, CH - 8, cap), F32),
            pltpu.VMEM((devices, 8, cap), F32),
            pltpu.VMEM((devices, CH - 8, cap), F32),
            pltpu.VMEM((CH * devices, 2 * cap), BF16),
            pltpu.VMEM((CH * devices, cap), F32),
            pltpu.VMEM((16, slots), F32),
            pltpu.VMEM((16, slots), F32),
            pltpu.VMEM((pixels, slots), F32),
            pltpu.VMEM((pixels, slots), F32),
            pltpu.VMEM((pixels, 2 * SB), BF16),
            pltpu.VMEM((pixels, SB), F32),
            pltpu.VMEM((pixels, SB), F32),
            pltpu.VMEM((CH * devices, 2 * slots), BF16),
            pltpu.VMEM((pixels, slots), BF16),
            pltpu.VMEM((pixels, slots), BF16),
            pltpu.SemaphoreType.DMA((2,)),
            pltpu.SemaphoreType.DMA((5,)),
            pltpu.SemaphoreType.DMA((5,)),
        ],
        compiler_params=pltpu.CompilerParams(collective_id=0, has_side_effects=True),
        name="step",
    )(list_length, list_owner.reshape(tiles, 1, slots), list_slot, target, splat_params)
    splat_grads = pl.pallas_call(
        scatter_kernel,
        in_specs=[smem, vmem, vmem, vmem],
        out_specs=pl.BlockSpec(memory_space=pl.ANY),
        out_shape=jax.ShapeDtypeStruct((CH, splats), F32),
        scratch_shapes=[
            pltpu.VMEM((total, 128), F32),
            pltpu.VMEM((CH, splats), F32),
            pltpu.SemaphoreType.DMA,
        ]
        + [pltpu.VMEM((rows, 128), F32)] * 4,
        name="accumulate",
    )(asked.reshape(-1), asked, incoming, coming)
    return (rendered, splat_grads)


def solution(mesh):
    in_specs = (
        P(None, ("row", "col")),
        P(("row", "col"), None, None),
        P(("row", "col"), None),
        P(("row", "col")),
        P(None, ("row", "col"), None),
    )
    out_specs = (P(None, ("row", "col"), None), P(None, ("row", "col")))
    return jax.shard_map(body, mesh=mesh, in_specs=in_specs, out_specs=out_specs, check_vma=False)
```

```python
import functools

import jax
import jax.numpy as jnp
from jax import lax
from jax.experimental import pallas as pl
from jax.experimental.pallas import tpu as pltpu
from jax.sharding import PartitionSpec as P

SIDE = 16
SB = 256
CH = 10
F32 = jnp.float32
BF16 = jnp.bfloat16
NT = (((1,), (1,)), ((), ()))
BLOCK = 512
LOG2E = 1.4426950408889634


def iota(shape, dim):
    return lax.broadcasted_iota(jnp.int32, shape, dim)


def split(x):
    high = x.astype(BF16)
    return high, (x - high.astype(F32)).astype(BF16)


def mm(a, b):
    return jnp.dot(a, b, preferred_element_type=F32)


def mm_nt(a, b):
    return lax.dot_general(a, b, NT, preferred_element_type=F32)


def one_hot(index, size):
    return jnp.where(iota((size, index.shape[1]), 0) == index, 1.0, 0.0).astype(BF16)


def step_kernel(
    length_ref, own_ref, slot_ref, target_ref, params_hbm, image_ref, asked_ref, incoming_ref, coming_ref,
    params_ref, table_ref, wide_ref, even_ref, odd_ref, lines_ref, live_ref, rank_ref, req_ref,
    found_ref, find_ref, replies_ref, reply_ref, outgoing_ref, going_ref, reply_both, sent_ref,
    vals, grads, falloff_ref, trans_ref, both_ref, shade_ref, after_ref, pack_ref, heavy_ref, light_ref,
    local_sem, send_sem, recv_sem,
):
    rows_on = lax.axis_size("row")
    cols_on = lax.axis_size("col")
    devices = rows_on * cols_on
    me = lax.axis_index("row") * cols_on + lax.axis_index("col")
    tiles, slots = slot_ref.shape
    cap = found_ref.shape[2]
    pixels = target_ref.shape[2]
    rows = table_ref.shape[0]
    others = pl.ds(0, devices - 1)

    def peer(k):
        return lax.rem(me + k, devices)

    def place_of(device):
        return (device // cols_on, lax.rem(device, cols_on))

    def push(device, source, target, phase):
        return pltpu.make_async_remote_copy(
            src_ref=source.at[device],
            dst_ref=target.at[me],
            send_sem=send_sem.at[phase],
            recv_sem=recv_sem.at[phase],
            device_id=place_of(device),
            device_id_type=pl.DeviceIdType.MESH,
        )

    def drain(source, target, phase):
        pltpu.make_async_copy(target.at[others], target.at[others], recv_sem.at[phase]).wait()
        pltpu.make_async_copy(source.at[others], source.at[others], send_sem.at[phase]).wait()

    barrier = pltpu.get_barrier_semaphore()

    @pl.loop(1, devices)
    def _(k):
        pl.semaphore_signal(
            barrier, inc=1, device_id=place_of(peer(k)), device_id_type=pl.DeviceIdType.MESH
        )

    load = pltpu.make_async_copy(params_hbm, params_ref, local_sem.at[0])
    load.start()

    strict = jnp.where(iota((SB, SB), 0) < iota((SB, SB), 1), 1.0, 0.0).astype(BF16)
    later = jnp.where(iota((SB, SB), 0) > iota((SB, SB), 1), 1.0, 0.0).astype(BF16)
    strict_twice = jnp.concatenate([strict, strict], axis=0)
    later_twice = jnp.concatenate([later, later], axis=0)
    count = jnp.zeros((devices, 1), F32)
    high = jnp.zeros((devices, cap), F32)
    low = jnp.zeros((devices, cap), F32)
    for tile in range(tiles):
        for j in range(slots // SB):
            part = slice(j * SB, (j + 1) * SB)
            owner = jnp.where(iota((1, SB), 1) + j * SB < length_ref[tile], own_ref[tile, :, part], -1)
            live_ref[tile, :, part] = owner
            mine = iota((devices, SB), 0) == owner
            ones = jnp.where(mine, 1.0, 0.0)
            ahead = mm(ones.astype(BF16), strict) + count
            rank = jnp.sum(ones * ahead, axis=0, keepdims=True).astype(jnp.int32)
            count = count + jnp.sum(ones, axis=1, keepdims=True)
            rank_ref[tile, :, part] = rank
            named = slot_ref[tile : tile + 1, part]
            places = one_hot(rank, cap)
            slot_high = (named >> 8).astype(F32)
            slot_low = ((named & 255) + 1).astype(F32)
            high = high + mm_nt(jnp.where(mine, slot_high, 0.0).astype(BF16), places)
            low = low + mm_nt(jnp.where(mine, slot_low, 0.0).astype(BF16), places)
    wanted = (high * 256.0 + low).astype(jnp.int32) - 1
    chunk = wanted >> (8 * BLOCK).bit_length() - 1
    line = (chunk & (rows // BLOCK - 1)) * BLOCK + (wanted & (BLOCK - 1))
    group = jnp.where(wanted < 0, -1, (wanted >> BLOCK.bit_length() - 1) & 7)
    filled = jnp.broadcast_to(count, (devices, 128)).astype(jnp.int32)
    for d in range(devices):
        req_ref[d, :, :cap] = line[d : d + 1]
        req_ref[d, :, cap : 2 * cap] = group[d : d + 1]
        req_ref[d, :, 2 * cap :] = filled[d : d + 1]
    pl.semaphore_wait(barrier, devices - 1)

    @pl.loop(1, devices)
    def _(k):
        push(peer(k), req_ref, asked_ref, 0).start()

    asked_ref[me] = req_ref[me]
    load.wait()
    wide_ref[...] = jnp.zeros_like(wide_ref)

    @pl.loop(0, rows // BLOCK)
    def _(j):
        for k in range(8):
            at = pl.ds(pl.multiple_of((j * 8 + k) * BLOCK, BLOCK), BLOCK)
            wide_ref[k * 16 : k * 16 + CH, :] = params_ref[:, at]
        table_ref[pl.ds(pl.multiple_of(j * BLOCK, BLOCK), BLOCK), :] = jnp.transpose(wide_ref[...])

    drain(req_ref, asked_ref, 0)
    move = pltpu.make_async_copy(asked_ref, lines_ref, local_sem.at[1])
    move.start()
    move.wait()

    eye = jnp.where(iota((128, 128), 0) == iota((128, 128), 1), 1.0, 0.0).astype(BF16)

    def fetch(source, held):
        for j in range(cap):
            held[j : j + 1, :] = table_ref[pl.ds(lines_ref[source, 0, j], 1), :]

    def pick(source, held):
        high, low = split(held[...])
        turned = mm_nt(eye, high) + mm_nt(eye, low)
        group = asked_ref[source, :, cap : 2 * cap]
        found = jnp.zeros((16, cap), F32)
        for q in range(8):
            found = found + jnp.where(group == q, turned[q * 16 : q * 16 + 16], 0.0)
        return found[:8], found[8:CH]

    def answer(source, held):
        found_ref[source], find_ref[source] = pick(source, held)
        push(source, found_ref, replies_ref, 1).start()
        push(source, find_ref, reply_ref, 2).start()

    fetch(peer(1), even_ref)

    @pl.loop(0, devices // 2 - 1)
    def _(p):
        fetch(peer(2 * p + 2), odd_ref)
        answer(peer(2 * p + 1), even_ref)
        fetch(peer(2 * p + 3), even_ref)
        answer(peer(2 * p + 2), odd_ref)

    answer(peer(devices - 1), even_ref)
    fetch(me, odd_ref)
    replies_ref[me], reply_ref[me] = pick(me, odd_ref)
    drain(found_ref, replies_ref, 1)
    drain(find_ref, reply_ref, 2)

    for ch in range(CH):
        part = slice(ch * devices, (ch + 1) * devices)
        reply_both[part, :cap], reply_both[part, cap:] = split(replies_ref[:, ch, :] if ch < 8 else reply_ref[:, ch - 8, :])
    sent_ref[...] = jnp.zeros_like(sent_ref)
    blocks = slots // SB
    centres = iota((SIDE, SB), 0).astype(F32) + 0.5
    side_rows = pixels // SIDE

    @pl.loop(0, tiles)
    def _(tile):
        length = length_ref[tile]
        mine = iota((devices, slots), 0) == live_ref[tile]
        places = one_hot(rank_ref[tile], cap)
        fetched = mm(reply_both[...], jnp.concatenate([places, places], axis=0))
        vals[...] = jnp.zeros_like(vals)
        live = jnp.where(iota((1, slots), 1) < length, 1.0, 0.0)
        for ch in range(CH):
            part = slice(ch * devices, (ch + 1) * devices)
            value = jnp.sum(jnp.where(mine, fetched[part], 0.0), axis=0, keepdims=True)
            if ch == 5:
                value = value * live
            row = ch if ch < 6 else ch + 2
            vals[row : row + 1, :] = value

        carry = jnp.zeros((pixels, 1), F32)
        image = jnp.zeros((pixels, 16), F32)
        image_light = jnp.zeros((pixels, 8), F32)
        for blk in range(blocks):
            at = slice(blk * SB, (blk + 1) * SB)
            dx = centres - vals[0:1, at]
            dy = centres - vals[1:2, at]
            ex = (-0.5 * LOG2E) * vals[2:3, at] * dx * dx
            ey = (-0.5 * LOG2E) * vals[4:5, at] * dy * dy
            bdy = -LOG2E * vals[3:4, at] * dy
            opacity = vals[5:6, at]
            for y in range(side_rows):
                rows_at = slice(y * SIDE, (y + 1) * SIDE)
                falloff = jnp.exp2(ex + ey[y : y + 1] + dx * bdy[y : y + 1])
                falloff_ref[rows_at, at] = falloff
                both_ref[rows_at, :SB], both_ref[rows_at, SB:] = split(jnp.log2(1.0 - opacity * falloff))
            total = mm(both_ref[...], strict_twice) + carry
            last = both_ref[:, SB - 128 : SB].astype(F32) + both_ref[:, 2 * SB - 128 :].astype(F32)
            carry = total[:, SB - 1 : SB] + last[:, 127:128]
            trans = jnp.exp2(total)
            trans_ref[:, at] = trans
            weight_high, weight_low = split(trans * (opacity * falloff_ref[:, at]))
            heavy_ref[:, at] = weight_high
            light_ref[:, at] = weight_low
            colour_high, colour_low = split(vals[8:16, at])
            image = image + mm_nt(weight_high, jnp.concatenate([colour_high, colour_low], axis=0))
            image_light = image_light + mm_nt(weight_low, colour_high)
        turned_image = jnp.transpose(image)
        rendered = turned_image[:8] + turned_image[8:] + jnp.transpose(image_light)
        for ch in range(4):
            image_ref[ch, pl.ds(tile, 1), :] = rendered[ch : ch + 1]
        wished = [target_ref[ch, pl.ds(tile, 1), :] for ch in range(4)]
        wished = jnp.concatenate(wished + [jnp.zeros((4, pixels), F32)], axis=0)
        grad_image = 2.0 * (rendered - wished)
        grad_high, grad_low = split(grad_image)
        grad_wide = grad_high.astype(F32)
        grad_rest = grad_image - grad_wide
        turned = jnp.transpose(jnp.concatenate([grad_wide, grad_wide, grad_rest, grad_image], axis=0))
        turned_parts = turned.astype(BF16)
        grad_both = jnp.concatenate([grad_high, grad_low], axis=0)

        spent = jnp.zeros((pixels, 1), F32)
        for blk in reversed(range(blocks)):
            at = slice(blk * SB, (blk + 1) * SB)
            mean_x, mean_y = vals[0:1, at], vals[1:2, at]
            conic_a, conic_b, conic_c = vals[2:3, at], vals[3:4, at], vals[4:5, at]
            opacity = vals[5:6, at]
            dx = centres - mean_x
            dy = centres - mean_y
            colours = vals[8:16, at]
            colour_wide = colours.astype(BF16).astype(F32)
            colour_parts = jnp.concatenate(
                [colour_wide, colours - colour_wide, colour_wide, jnp.zeros_like(colours)], axis=0
            ).astype(BF16)
            shading = mm(turned_parts, colour_parts)
            shade_ref[...] = shading
            colour_grads = mm(grad_both, heavy_ref[:, at])
            grads[8:16, at] = colour_grads[:8] + colour_grads[8:] + mm(grad_high, light_ref[:, at])
            gain = trans_ref[:, at] * (opacity * falloff_ref[:, at]) * shading
            both_ref[:, :SB], both_ref[:, SB:] = split(gain)
            after = mm(both_ref[...], later_twice) + spent
            spent = after[:, 0:1] + gain[:, 0:1]
            after_ref[...] = after
            moment0 = jnp.zeros((SIDE, SB), F32)
            moment1 = moment0
            moment2 = moment0
            for y in range(side_rows):
                rows_at = slice(y * SIDE, (y + 1) * SIDE)
                falloff = falloff_ref[rows_at, at]
                grad_alpha = trans_ref[rows_at, at] * shade_ref[rows_at, :] - after_ref[rows_at, :] / (
                    1.0 - opacity * falloff
                )
                opaque = grad_alpha * falloff
                moment0 = moment0 + opaque
                lever = opaque * dy[y : y + 1]
                moment1 = moment1 + lever
                moment2 = moment2 + lever * dy[y : y + 1]
            across = moment0 * dx
            sum_x = jnp.sum(across, axis=0, keepdims=True)
            sum_y = jnp.sum(moment1, axis=0, keepdims=True)
            grads[0:1, at] = opacity * (conic_a * sum_x + conic_b * sum_y)
            grads[1:2, at] = opacity * (conic_c * sum_y + conic_b * sum_x)
            grads[2:3, at] = -0.5 * opacity * jnp.sum(across * dx, axis=0, keepdims=True)
            grads[3:4, at] = -opacity * jnp.sum(moment1 * dx, axis=0, keepdims=True)
            grads[4:5, at] = -0.5 * opacity * jnp.sum(moment2, axis=0, keepdims=True)
            grads[5:6, at] = jnp.sum(moment0, axis=0, keepdims=True) * live[:, at]

        for ch in range(CH):
            part = slice(ch * devices, (ch + 1) * devices)
            row = ch if ch < 6 else ch + 2
            high, low = split(jnp.where(mine, grads[row : row + 1, :], 0.0))
            pack_ref[part, :slots] = high
            pack_ref[part, slots:] = low
        sent = mm_nt(pack_ref[...], jnp.concatenate([places, places], axis=1))

        sent_ref[...] += sent

    for ch in range(CH):
        part = slice(ch * devices, (ch + 1) * devices)
        if ch < 8:
            outgoing_ref[:, ch, :] = sent_ref[part, :]
        else:
            going_ref[:, ch - 8, :] = sent_ref[part, :]

    @pl.loop(1, devices)
    def _(k):
        push(peer(k), outgoing_ref, incoming_ref, 3).start()
        push(peer(k), going_ref, coming_ref, 4).start()

    incoming_ref[me] = outgoing_ref[me]
    coming_ref[me] = going_ref[me]
    drain(outgoing_ref, incoming_ref, 3)
    drain(going_ref, coming_ref, 4)


def scatter_kernel(
    line_ref, ask_ref, grad_ref, rest_ref, seen_ref, image_ref, out_hbm, wide_ref, out_ref, out_sem, *banks
):
    rows = banks[0].shape[0]
    devices, _, cap = grad_ref.shape
    share = rows // devices
    burst = 32
    image_ref[...] = seen_ref[...]

    @pl.loop(0, devices // 2)
    def _(p):
        wides = []
        for s in (2 * p, 2 * p + 1):
            group = ask_ref[s, :, cap : 2 * cap]
            parts = [grad_ref[s], rest_ref[s], jnp.zeros((16 - CH, cap), F32)]
            grad = jnp.concatenate(parts, axis=0)
            wides.append(jnp.concatenate([jnp.where(group == k, grad, 0.0) for k in range(8)], axis=0))
        lines = [jnp.transpose(wide) for wide in wides]
        at = pl.ds(pl.multiple_of(p * 2 * share, 2 * share), 2 * share)
        for bank in banks:
            bank[at, :] = jnp.zeros((2 * share, 128), F32)
        for k, line in enumerate(lines):
            wide_ref[pl.ds(pl.multiple_of((2 * p + k) * cap, cap), cap), :] = line

    @pl.loop(0, devices)
    def _(s):
        base = s * (line_ref.shape[0] // devices)

        @pl.loop(0, (line_ref[base + 2 * cap] + burst - 1) // burst)
        def _(j):
            first = j * burst
            lines = wide_ref.at[pl.ds(pl.multiple_of(s * cap + first, burst), burst), :]
            for u in range(burst):
                bank = banks[u % len(banks)]
                at = pl.ds(line_ref[base + first + u], 1)
                bank[at, :] = bank[at, :] + lines[u : u + 1, :]

    def leave(j):
        to = pl.ds(pl.multiple_of(j * 8 * BLOCK, 8 * BLOCK), 8 * BLOCK)
        return pltpu.make_async_copy(out_ref.at[:, to], out_hbm.at[:, to], out_sem)

    @pl.loop(0, rows // BLOCK, unroll=2)
    def _(j):
        at = pl.ds(pl.multiple_of(j * BLOCK, BLOCK), BLOCK)
        total = banks[0][at, :]
        for bank in banks[1:]:
            total = total + bank[at, :]
        turned = jnp.transpose(total)
        for k in range(8):
            to = pl.ds(pl.multiple_of((j * 8 + k) * BLOCK, BLOCK), BLOCK)
            out_ref[:, to] = turned[k * 16 : k * 16 + CH]
        leave(j).start()

    pltpu.make_async_copy(out_ref, out_hbm, out_sem).wait()


def body(splat_params, list_owner, list_slot, list_length, target):
    devices = lax.axis_size(("row", "col"))
    tiles, slots = list_slot.shape
    entries = tiles * slots
    splats = splat_params.shape[1]
    pixels = target.shape[2]
    cap = 2 * entries // devices
    total = devices * cap
    rows = splats // 8
    smem = pl.BlockSpec(memory_space=pltpu.SMEM)
    vmem = pl.BlockSpec(memory_space=pltpu.VMEM)
    seen, asked, incoming, coming = pl.pallas_call(
        step_kernel,
        in_specs=[smem, vmem, vmem, vmem, pl.BlockSpec(memory_space=pl.ANY)],
        out_specs=(vmem, vmem, vmem, vmem),
        out_shape=(
            jax.ShapeDtypeStruct((4, tiles, pixels), F32),
            jax.ShapeDtypeStruct((devices, 1, 2 * cap + 128), jnp.int32),
            jax.ShapeDtypeStruct((devices, 8, cap), F32),
            jax.ShapeDtypeStruct((devices, CH - 8, cap), F32),
        ),
        scratch_shapes=[
            pltpu.VMEM((CH, splats), F32),
            pltpu.VMEM((rows, 128), F32),
            pltpu.VMEM((128, BLOCK), F32),
            pltpu.VMEM((cap, 128), F32),
            pltpu.VMEM((cap, 128), F32),
            pltpu.SMEM((devices, 1, 2 * cap + 128), jnp.int32),
            pltpu.VMEM((tiles, 1, slots), jnp.int32),
            pltpu.VMEM((tiles, 1, slots), jnp.int32),
            pltpu.VMEM((devices, 1, 2 * cap + 128), jnp.int32),
            pltpu.VMEM((devices, 8, cap), F32),
            pltpu.VMEM((devices, CH - 8, cap), F32),
            pltpu.VMEM((devices, 8, cap), F32),
            pltpu.VMEM((devices, CH - 8, cap), F32),
            pltpu.VMEM((devices, 8, cap), F32),
            pltpu.VMEM((devices, CH - 8, cap), F32),
            pltpu.VMEM((CH * devices, 2 * cap), BF16),
            pltpu.VMEM((CH * devices, cap), F32),
            pltpu.VMEM((16, slots), F32),
            pltpu.VMEM((16, slots), F32),
            pltpu.VMEM((pixels, slots), F32),
            pltpu.VMEM((pixels, slots), F32),
            pltpu.VMEM((pixels, 2 * SB), BF16),
            pltpu.VMEM((pixels, SB), F32),
            pltpu.VMEM((pixels, SB), F32),
            pltpu.VMEM((CH * devices, 2 * slots), BF16),
            pltpu.VMEM((pixels, slots), BF16),
            pltpu.VMEM((pixels, slots), BF16),
            pltpu.SemaphoreType.DMA((2,)),
            pltpu.SemaphoreType.DMA((5,)),
            pltpu.SemaphoreType.DMA((5,)),
        ],
        compiler_params=pltpu.CompilerParams(collective_id=0, has_side_effects=True),
        name="step",
    )(list_length, list_owner.reshape(tiles, 1, slots), list_slot, target, splat_params)
    rendered, splat_grads = pl.pallas_call(
        scatter_kernel,
        in_specs=[smem, vmem, vmem, vmem, vmem],
        out_specs=(vmem, pl.BlockSpec(memory_space=pl.ANY)),
        out_shape=(
            jax.ShapeDtypeStruct((4, tiles, pixels), F32),
            jax.ShapeDtypeStruct((CH, splats), F32),
        ),
        scratch_shapes=[
            pltpu.VMEM((total, 128), F32),
            pltpu.VMEM((CH, splats), F32),
            pltpu.SemaphoreType.DMA,
        ]
        + [pltpu.VMEM((rows, 128), F32)] * 4,
        name="accumulate",
    )(asked.reshape(-1), asked, incoming, coming, seen)
    return (rendered, splat_grads)


def solution(mesh):
    in_specs = (
        P(None, ("row", "col")),
        P(("row", "col"), None, None),
        P(("row", "col"), None),
        P(("row", "col")),
        P(None, ("row", "col"), None),
    )
    out_specs = (P(None, ("row", "col"), None), P(None, ("row", "col")))
    return jax.shard_map(body, mesh=mesh, in_specs=in_specs, out_specs=out_specs, check_vma=False)
```
